128 devices in a mesh: req: 32 (over x, z, core), mlp: 4 (over y).
Axes of the slice: x: 4, y: 4, z: 4, core: 2. Of those that a mesh axis runs over, the one named last changes fastest.
Arguments:
- tokens: bfloat16 [4096, 3584], P('req'), may hold values from -40 to 40
- segment_ids: int32 [32, 128], P('req'), may hold values from 0 to 3, never falling along the last dimension, each value on 1 to 64 neighbouring positions
- past_len: int32 [32, 4], P('req'), may hold values from 0 to 2047
- page_table: int32 [32, 64], P('req'), may hold values from 0 to 63, each once within a row
- migrate_pages: int32 [32, 32, 1], P('req'), may hold values from 0 to 31
- pooled_key_cache: bfloat16 [1024, 64, 1024], P('req', None, 'mlp'), may hold values from -6 to 6
- pooled_value_cache: bfloat16 [1024, 64, 1024], P('req', None, 'mlp'), may hold values from -6 to 6
- attn_gain: float32 [3584], replicated, may hold values from 0.25 to 1.75
- w_query: bfloat16 [3584, 2048], P(None, 'mlp'), may hold values from -0.09375 to 0.09375
- key_matrix: bfloat16 [3584, 1024], P(None, 'mlp'), may hold values from -0.09375 to 0.09375
- value_matrix: bfloat16 [3584, 1024], P(None, 'mlp'), may hold values from -0.09375 to 0.09375
- w_out: bfloat16 [2048, 3584], P('mlp'), may hold values from -1 to 1
- post_attn_gain: float32 [3584], replicated, may hold values from 0.25 to 1.75
- ffw_gain: float32 [3584], replicated, may hold values from 0.25 to 1.75
- w_gate: bfloat16 [3584, 14336], P(None, 'req'), may hold values from -0.09375 to 0.09375
- w_up: bfloat16 [3584, 14336], P(None, 'req'), may hold values from -0.09375 to 0.09375
- w_down: bfloat16 [14336, 3584], P('req'), may hold values from -1 to 1
- post_ffw_gain: float32 [3584], replicated, may hold values from 0.25 to 1.75
Outputs:
- mixed: bfloat16 [4096, 3584], P(('req', 'mlp'))
- written_key_rows: bfloat16 [4096, 1024], P('req', 'mlp')
- written_value_rows: bfloat16 [4096, 1024], P('req', 'mlp')
The draws below stay inside these ranges and needn't reach their ends.
Inputs may be any that keep to these rules, and one draw needn't show every extreme that they name: `segment_ids`: in each row the requests 0 to 3 appear in order; each request has 1 to 64 new tokens, and some request exactly 64. `page_table`: each row is a permutation; every page of the owner's list (own pool and received pages) lies in exactly one request's window. `migrate_pages`: entry [s, d, m] names a page of owner s's pool.
All inputs are finite; a program needn't handle non-finite values.
Results may differ from the reference program's by a relative error of at most 0.015.
Values may be sent and summed in bfloat16 or wider, within the bound.
No kernel may reach another device: no remote copies, remote signals or barrier semaphores. Data moves between devices by JAX's collectives and lax.ppermute only.
A program may use at most 128 MiB of HBM per device.

```python
import math
import jax
import jax.numpy as jnp
import numpy as np
from jax import lax

MODEL_WIDTH = 3584
FF = 14336
HEAD_SIZE = 256
QUERY_HEAD_COUNT = 8
KEY_VALUE_HEADS = 4
WINDOW_LENGTH = 1024
PAGE_POSITIONS = 64
OWNED_REQUESTS = 4
MIGP = 1
OWNED_TOKENS = 128
SEG_MOST = 64
WIN_PAGES = 16
POOL_PAGES = 32
TOKEN_TOTAL = 4096
N_REQ = 32


def spread_weight(key, rows, cols):
    first, second = jax.random.split(key)
    base = jnp.clip(jax.random.normal(first, (rows, cols), jnp.float32), -4.0, 4.0)
    column = jnp.exp(jax.random.uniform(second, (1, cols), jnp.float32, -1.15, 1.15))
    return (base * column * float(rows) ** (-0.5)).astype(jnp.bfloat16)


def draw_tokens(key, part):
    first, second, third = jax.random.split(key, 3)
    row_scale = jnp.exp(jax.random.uniform(second, (TOKEN_TOTAL, 1), jnp.float32, -1.15, 1.15))
    col_scale = jnp.exp(jax.random.uniform(third, (1, MODEL_WIDTH), jnp.float32, -1.15, 1.15))
    base = jnp.clip(jax.random.normal(first, (TOKEN_TOTAL, MODEL_WIDTH), jnp.float32), -4.0, 4.0)
    return (base * row_scale * col_scale).astype(jnp.bfloat16)


def draw_w_out(key, part):
    return spread_weight(jax.random.fold_in(key, 11), QUERY_HEAD_COUNT * HEAD_SIZE, MODEL_WIDTH)


def draw_w_down(key, part):
    return spread_weight(jax.random.fold_in(key, 23), FF, MODEL_WIDTH)


def touch_ends(entries, own_key, least, largest):
    index_at = [jax.random.randint(jax.random.fold_in(own_key, axis), (), 0, length) for axis, length in enumerate(entries.shape)]
    longest = entries.shape.index(max(entries.shape))
    neighbour = index_at[:longest] + [(index_at[longest] + 1) % entries.shape[longest]] + index_at[longest + 1:]
    return entries.at[tuple(index_at)].set(least).at[tuple(neighbour)].set(largest)


def levels(stream_key, extent, pieces, low, largest):
    level, own = 1.0, jax.random.fold_in(stream_key, 6)
    for position, parts in pieces:
        heights = jnp.exp(jax.random.uniform(jax.random.fold_in(own, position), (parts,), jnp.float32, low / len(pieces), largest / len(pieces)))
        level = level * jnp.repeat(heights, extent[position] // parts).reshape([-1 if axis == position else 1 for axis in range(len(extent))])
    return level


def profile(amount, total, reach, skew):
    portions = [(1 << 20) // math.isqrt(grade ** skew) + 1 for grade in range(2, amount + 1)]
    rest, holding = total - reach - (amount - 1), [1] * (amount - 1)
    while rest > 0:
        candidates = [i for i in range(amount - 1) if holding[i] < reach]
        mass, budget = sum([portions[i] for i in candidates]), rest
        for i in candidates:
            extra = min(reach - holding[i], max(1, budget * portions[i] // mass), rest)
            holding[i] = holding[i] + extra
            rest = rest - extra
    return np.array([reach] + holding)


def uneven(rng, number_of, total, limit, lean):
    if number_of == 2:
        one = jax.random.randint(rng, (), max(1, total - limit), min(limit, total - 1) + 1)
        return jnp.stack([one, total - one])
    lengths = jnp.asarray(profile(number_of, total, limit, lean), jnp.int32)
    pairs = (number_of - 1) // 2
    donor, receiver = lengths[1:1 + 2 * pairs:2], lengths[2:2 + 2 * pairs:2]
    slack = jnp.minimum(donor - 1, limit - receiver)
    passed = jax.random.randint(jax.random.fold_in(rng, 1), (pairs,), 0, 1 << 20) % (slack + 1)
    lengths = lengths.at[1:1 + 2 * pairs:2].set(donor - passed).at[2:2 + 2 * pairs:2].set(receiver + passed)
    return lengths[jax.random.permutation(jax.random.fold_in(rng, 2), number_of)]


def bell_draw(key, shape, scale, reach, shards=(), held_as=jnp.bfloat16):
    entries = jax.random.normal(key, shape, jnp.float32) * scale
    if len(shards) > 0:
        entries = levels(key, shape, shards, -0.22, 0.18) * entries
    return jnp.clip(entries, min=-reach, max=reach).astype(held_as)


def setup_inputs(seed: int = 0) -> dict:
    streams_of = jax.random.split(jax.random.key(seed), 19)
    return {
        "tokens": draw_tokens(jax.random.fold_in(streams_of[18], 71), 0),
        "segment_ids": jax.vmap(lambda own: jnp.searchsorted(jnp.cumsum(uneven(own, OWNED_REQUESTS, OWNED_TOKENS, SEG_MOST, 1)), jnp.arange(OWNED_TOKENS), side="right"))(jax.random.split(streams_of[1], N_REQ)).reshape((N_REQ, OWNED_TOKENS)).astype(jnp.int32),
        "past_len": touch_ends(jax.random.randint(streams_of[2], (N_REQ, OWNED_REQUESTS), 0, 2 * WINDOW_LENGTH), jax.random.fold_in(streams_of[2], 1), 0, (2 * WINDOW_LENGTH) - 1).astype(jnp.int32),
        "page_table": jax.vmap(lambda own: jax.random.permutation(own, OWNED_REQUESTS * WIN_PAGES))(jax.random.split(streams_of[3], N_REQ)).reshape((N_REQ, OWNED_REQUESTS * WIN_PAGES)).astype(jnp.int32),
        "migrate_pages": touch_ends(jax.random.randint(streams_of[4], (N_REQ, N_REQ, MIGP), 0, POOL_PAGES), jax.random.fold_in(streams_of[4], 1), 0, POOL_PAGES - 1).astype(jnp.int32),
        "pooled_key_cache": bell_draw(streams_of[5], (N_REQ * POOL_PAGES, PAGE_POSITIONS, KEY_VALUE_HEADS * HEAD_SIZE), 1.0, 6.0, ((0, 32), (2, 4))),
        "pooled_value_cache": bell_draw(streams_of[6], (N_REQ * POOL_PAGES, PAGE_POSITIONS, KEY_VALUE_HEADS * HEAD_SIZE), 1.0, 6.0, ((0, 32), (2, 4))),
        "attn_gain": jnp.clip(1.0 + 0.15 * jax.random.normal(streams_of[7], (MODEL_WIDTH,), jnp.float32), 0.25, 1.75),
        "w_query": bell_draw(streams_of[8], (MODEL_WIDTH, QUERY_HEAD_COUNT * HEAD_SIZE), MODEL_WIDTH ** -0.5, 0.09375, ((1, 4),)),
        "key_matrix": bell_draw(streams_of[9], (MODEL_WIDTH, KEY_VALUE_HEADS * HEAD_SIZE), MODEL_WIDTH ** -0.5, 0.09375, ((1, 4),)),
        "value_matrix": bell_draw(streams_of[10], (MODEL_WIDTH, KEY_VALUE_HEADS * HEAD_SIZE), MODEL_WIDTH ** -0.5, 0.09375, ((1, 4),)),
        "w_out": draw_w_out(jax.random.fold_in(streams_of[18], 71), 0),
        "post_attn_gain": jnp.clip(1.0 + 0.15 * jax.random.normal(streams_of[12], (MODEL_WIDTH,), jnp.float32), 0.25, 1.75),
        "ffw_gain": jnp.clip(1.0 + 0.15 * jax.random.normal(streams_of[13], (MODEL_WIDTH,), jnp.float32), 0.25, 1.75),
        "w_gate": bell_draw(streams_of[14], (MODEL_WIDTH, FF), MODEL_WIDTH ** -0.5, 0.09375, ((1, 32),)),
        "w_up": bell_draw(streams_of[15], (MODEL_WIDTH, FF), MODEL_WIDTH ** -0.5, 0.09375, ((1, 32),)),
        "w_down": draw_w_down(jax.random.fold_in(streams_of[18], 71), 0),
        "post_ffw_gain": jnp.clip(1.0 + 0.15 * jax.random.normal(streams_of[17], (MODEL_WIDTH,), jnp.float32), 0.25, 1.75),
    }


SOFT_CAP = 50.0
NORM_EPS = 1e-06
ROPE_BASE = 10000.0

def rms_scale(values, gain):
    return values * lax.rsqrt(lax.optimization_barrier(jnp.mean(values * values, axis=-1, keepdims=True)) + NORM_EPS) * gain

def apply_rotary(vectors, token_positions):
    width = vectors.shape[-1]
    half = width // 2
    frequency = ROPE_BASE ** (-jnp.arange(half, dtype=jnp.float32) * (2.0 / width))
    angles = token_positions.astype(jnp.float32)[:, None] * frequency[None, :]
    cosine = jnp.cos(angles)[:, None, :]
    sine = jnp.sin(angles)[:, None, :]
    first = vectors[..., :half]
    second = vectors[..., half:]
    return jnp.concatenate([first * cosine - second * sine, second * cosine + first * sine], axis=-1)

def token_layout(segment, past):
    requests = jnp.arange(past.shape[0], dtype=jnp.int32)
    member = segment[:, None] == requests[None, :]
    firsts = lax.optimization_barrier(jnp.sum((segment[:, None] < requests[None, :]).astype(jnp.int32), axis=0))
    offsets = jnp.arange(segment.shape[0], dtype=jnp.int32) - lax.optimization_barrier(jnp.sum(jnp.where(member, firsts[None, :], 0), axis=1))
    token_positions = lax.optimization_barrier(jnp.sum(jnp.where(member, past[None, :], 0), axis=1)) + offsets
    return (offsets.astype(jnp.int32), token_positions.astype(jnp.int32))

def visibility(segment, offsets, past, window):
    count_req = past.shape[0]
    requests = jnp.arange(count_req, dtype=jnp.int32)
    slots = jnp.arange(count_req * window, dtype=jnp.int32)
    slot_req = slots // window
    slot_pos = slots % window
    slot_past = lax.optimization_barrier(jnp.sum(jnp.where(slot_req[:, None] == requests[None, :], past[None, :], 0), axis=1))
    cached = (segment[:, None] == slot_req[None, :]) & (slot_pos[None, :] > offsets[:, None]) & (slot_pos[None, :] >= window - slot_past[None, :])
    order = jnp.arange(segment.shape[0], dtype=jnp.int32)
    fresh = (segment[:, None] == segment[None, :]) & (order[None, :] <= order[:, None])
    return (cached, fresh)

def reference(tokens, segment_ids, past_len, page_table, migrate_pages, pooled_key_cache, pooled_value_cache, attn_gain, w_query, key_matrix, value_matrix, w_out, post_attn_gain, ffw_gain, w_gate, w_up, w_down, post_ffw_gain):
    query_group = QUERY_HEAD_COUNT // KEY_VALUE_HEADS
    scale = float(HEAD_SIZE) ** (-0.5)

    def one_owner(owner):
        rows = lax.dynamic_slice_in_dim(tokens, owner * OWNED_TOKENS, OWNED_TOKENS, 0).astype(jnp.float32)
        segment = segment_ids[owner]
        past = past_len[owner]
        offsets, token_positions = token_layout(segment, past)
        sources = (jnp.arange(N_REQ, dtype=jnp.int32)[:, None] * POOL_PAGES + migrate_pages[:, owner, :]).reshape(-1).astype(jnp.int32)
        page_lookup = page_table[owner]

        def window_of(cache):
            local = lax.dynamic_slice_in_dim(cache, owner * POOL_PAGES, POOL_PAGES, 0)
            listed_pages = jnp.concatenate([local, jnp.take(cache, sources, axis=0)], axis=0)
            return jnp.take(listed_pages, page_lookup, axis=0).reshape(OWNED_REQUESTS * WINDOW_LENGTH, KEY_VALUE_HEADS, HEAD_SIZE)
        window_keys = window_of(pooled_key_cache)
        window_values = window_of(pooled_value_cache)
        normalized_input = rms_scale(rows, attn_gain).astype(jnp.bfloat16)
        query_rows = apply_rotary(jnp.dot(normalized_input, w_query, preferred_element_type=jnp.float32).reshape(OWNED_TOKENS, QUERY_HEAD_COUNT, HEAD_SIZE), token_positions).astype(jnp.bfloat16)
        incoming_keys = apply_rotary(jnp.dot(normalized_input, key_matrix, preferred_element_type=jnp.float32).reshape(OWNED_TOKENS, KEY_VALUE_HEADS, HEAD_SIZE), token_positions).astype(jnp.bfloat16)
        incoming_values = jnp.dot(normalized_input, value_matrix, preferred_element_type=jnp.float32).astype(jnp.bfloat16).reshape(OWNED_TOKENS, KEY_VALUE_HEADS, HEAD_SIZE)
        all_keys = jnp.concatenate([window_keys, incoming_keys], axis=0).astype(jnp.float32)
        all_values = jnp.concatenate([window_values, incoming_values], axis=0).astype(jnp.float32)
        grouped_queries = query_rows.reshape(OWNED_TOKENS, KEY_VALUE_HEADS, query_group, HEAD_SIZE).astype(jnp.float32)
        scores = jnp.einsum('tkgd,skd->tkgs', grouped_queries, all_keys)
        capped = SOFT_CAP * jnp.tanh(scores * (scale / SOFT_CAP))
        cached, fresh = visibility(segment, offsets, past, WINDOW_LENGTH)
        visible = jnp.concatenate([cached, fresh], axis=1)
        weights = jnp.where(visible[:, None, None, :], jnp.exp(capped), jnp.float32(0.0))
        probs = (weights / lax.optimization_barrier(jnp.sum(weights, axis=-1, keepdims=True))).astype(jnp.bfloat16)
        attention = jnp.einsum('tkgs,skd->tkgd', probs.astype(jnp.float32), all_values).astype(jnp.bfloat16).reshape(OWNED_TOKENS, QUERY_HEAD_COUNT * HEAD_SIZE)
        attn_out = jnp.dot(attention, w_out, preferred_element_type=jnp.float32)
        residual_stream = rows + rms_scale(attn_out, post_attn_gain)
        feedforward_input = rms_scale(residual_stream, ffw_gain).astype(jnp.bfloat16)
        return (residual_stream, feedforward_input, incoming_keys.reshape(OWNED_TOKENS, KEY_VALUE_HEADS * HEAD_SIZE), incoming_values.reshape(OWNED_TOKENS, KEY_VALUE_HEADS * HEAD_SIZE))
    residual_stream, feedforward_input, written_key_rows, written_value_rows = lax.map(one_owner, jnp.arange(N_REQ, dtype=jnp.int32))
    residual_stream = residual_stream.reshape(TOKEN_TOTAL, MODEL_WIDTH)
    feedforward_input = feedforward_input.reshape(TOKEN_TOTAL, MODEL_WIDTH)
    block_width = FF // N_REQ

    def add_block(total, index):
        gate_part = jnp.dot(feedforward_input, lax.dynamic_slice_in_dim(w_gate, index * block_width, block_width, 1), preferred_element_type=jnp.float32)
        up_part = jnp.dot(feedforward_input, lax.dynamic_slice_in_dim(w_up, index * block_width, block_width, 1), preferred_element_type=jnp.float32)
        hidden = (jax.nn.gelu(gate_part, approximate=True) * up_part).astype(jnp.bfloat16)
        product = jnp.dot(hidden, lax.dynamic_slice_in_dim(w_down, index * block_width, block_width, 0), preferred_element_type=jnp.float32).astype(jnp.bfloat16)
        return (total + lax.optimization_barrier(product).astype(jnp.float32), None)
    ffw_out, _ = lax.scan(add_block, jnp.zeros((TOKEN_TOTAL, MODEL_WIDTH), jnp.float32), jnp.arange(N_REQ, dtype=jnp.int32))
    mixed = (residual_stream + rms_scale(ffw_out, post_ffw_gain)).astype(jnp.bfloat16)
    return (mixed, written_key_rows.reshape(TOKEN_TOTAL, KEY_VALUE_HEADS * HEAD_SIZE), written_value_rows.reshape(TOKEN_TOTAL, KEY_VALUE_HEADS * HEAD_SIZE))
```

```python
import jax
import jax.numpy as jnp
from jax import lax
from jax.experimental import pallas as pl
from jax.experimental.pallas import tpu as pltpu
from jax.sharding import Mesh, PartitionSpec as P

HEAD_SIZE = 256
WINDOW_LENGTH = 1024
PAGE = 64
WIN_PAGES = 16
OWNERS = 32
POOL = 32
HEADS = 2
ROWS = 32

SOFT_CAP = 50.0
NORM_EPS = 1e-06
ROPE_BASE = 10000.0

BF16 = jnp.bfloat16
F32 = jnp.float32

REQ = ("x", "z", "core")


def rms_scale(values, gain):
    return values * lax.rsqrt(jnp.mean(values * values, axis=-1, keepdims=True) + NORM_EPS) * gain


def apply_rotary(vectors, token_positions):
    half = HEAD_SIZE // 2
    frequency = ROPE_BASE ** (-jnp.arange(half, dtype=F32) * (2.0 / HEAD_SIZE))
    angles = token_positions.astype(F32)[:, None] * frequency[None, :]
    cosine = jnp.cos(angles)[:, None, :]
    sine = jnp.sin(angles)[:, None, :]
    first = vectors[..., :half]
    second = vectors[..., half:]
    return jnp.concatenate(
        [first * cosine - second * sine, second * cosine + first * sine], axis=-1
    )


def token_layout(segment, past):
    requests = jnp.arange(past.shape[0], dtype=jnp.int32)
    member = segment[:, None] == requests[None, :]
    firsts = jnp.sum((segment[:, None] < requests[None, :]).astype(jnp.int32), axis=0)
    offsets = jnp.arange(segment.shape[0], dtype=jnp.int32) - jnp.sum(
        jnp.where(member, firsts[None, :], 0), axis=1
    )
    token_positions = jnp.sum(jnp.where(member, past[None, :], 0), axis=1) + offsets
    return (offsets, token_positions)


def chip_shift(first, k):
    pairs = []
    for x in range(4):
        for z in range(4):
            for c in range(2):
                if (c == 0) == first:
                    to = ((x + k) % 4, z)
                else:
                    to = (x, (z + k) % 4)
                pairs.append(((x * 4 + z) * 2 + c, (to[0] * 4 + to[1]) * 2 + c))
    return pairs


def shift(value, first, k):
    return lax.ppermute(value, REQ, chip_shift(first, k % 4))


def pick_pages_kernel(pages_ref, keys_ref, values_ref, out_ref, sems):
    copies = []
    for d in range(OWNERS):
        page = pages_ref[d]
        copies.append(pltpu.make_async_copy(keys_ref.at[page], out_ref.at[d, 0], sems.at[d, 0]))
        copies.append(pltpu.make_async_copy(values_ref.at[page], out_ref.at[d, 1], sems.at[d, 1]))
    for copy in copies:
        copy.start()
    for copy in copies:
        copy.wait()


def pick_pages(pages, keys, values):
    return pl.pallas_call(
        pick_pages_kernel,
        out_shape=jax.ShapeDtypeStruct((OWNERS, 2, PAGE, HEAD_SIZE), BF16),
        grid_spec=pltpu.PrefetchScalarGridSpec(
            num_scalar_prefetch=1,
            grid=(),
            in_specs=[pl.BlockSpec(memory_space=pl.ANY)] * 2,
            out_specs=pl.BlockSpec(memory_space=pl.ANY),
            scratch_shapes=[pltpu.SemaphoreType.DMA((OWNERS, 2))],
        ),
        name="pick_pages",
    )(pages, keys, values)


def weights_of(query, keys, visible):
    scores = lax.dot_general(
        query, keys, (((1,), (1,)), ((), ())), preferred_element_type=F32
    )
    raw = jnp.exp(SOFT_CAP * jnp.tanh(scores * (1.0 / (16.0 * SOFT_CAP))))
    return jnp.where(visible, raw, 0.0)


def attend(query_ref, keys, values, visible, acc_ref, total_ref):
    for h in range(HEADS):
        weight = weights_of(query_ref[h], keys, visible)
        total_ref[h] += jnp.broadcast_to(
            jnp.sum(weight, axis=-1, keepdims=True), total_ref.shape[1:]
        )
        acc_ref[h] += jnp.dot(weight.astype(BF16), values, preferred_element_type=F32)


STEP_PAGES = 8
STEP = STEP_PAGES * PAGE


def own_kernel(low_ref, high_ref, order_ref, seg_row_ref, query_ref, new_keys_ref, new_values_ref,
               code_ref, keys_ref, values_ref, acc_ref, total_ref):
    acc_ref[...] = jnp.zeros_like(acc_ref)
    total_ref[...] = jnp.zeros_like(total_ref)
    low, high, order = low_ref[...], high_ref[...], order_ref[...]
    count = order.shape[0]
    column = lax.broadcasted_iota(jnp.int32, (count, count), 1)
    same = lax.div(high, 4096) == seg_row_ref[...]
    attend(query_ref, new_keys_ref[...], new_values_ref[...], same & (column <= order), acc_ref, total_ref)
    for b in range(POOL // STEP_PAGES):
        keys = keys_ref[b * STEP_PAGES:(b + 1) * STEP_PAGES].reshape(STEP, HEAD_SIZE)
        values = values_ref[b * STEP_PAGES:(b + 1) * STEP_PAGES].reshape(STEP, HEAD_SIZE)
        code = code_ref[:, b * STEP:(b + 1) * STEP]
        attend(query_ref, keys, values, (code > low) & (code < high), acc_ref, total_ref)


def own_attention(low, high, order, seg_row, query, new_keys, new_values, code, keys, values):
    vmem = pl.BlockSpec(memory_space=pltpu.VMEM)
    return pl.pallas_call(
        own_kernel,
        out_shape=(
            jax.ShapeDtypeStruct((HEADS, 128, HEAD_SIZE), F32),
            jax.ShapeDtypeStruct((HEADS, 128, 128), F32),
        ),
        in_specs=[vmem] * 10,
        out_specs=(vmem, vmem),
        cost_estimate=pl.CostEstimate(
            flops=4 * 256 * 2176 * 256, transcendentals=2 * 256 * 2176, bytes_accessed=3_000_000
        ),
        name="own_attention",
    )(low, high, order, seg_row, query, new_keys, new_values, code, keys, values)


def far_kernel(low_ref, high_ref, query_ref, code_ref, pages_ref, acc_in_ref, total_in_ref, w_ref,
               out_ref, acc_ref, total_ref):
    acc_ref[...] = acc_in_ref[...]
    total_ref[...] = total_in_ref[...]
    low, high = low_ref[...], high_ref[...]
    for b in range(OWNERS // STEP_PAGES):
        keys = pages_ref[b * STEP_PAGES:(b + 1) * STEP_PAGES, 0].reshape(STEP, HEAD_SIZE)
        values = pages_ref[b * STEP_PAGES:(b + 1) * STEP_PAGES, 1].reshape(STEP, HEAD_SIZE)
        code = code_ref[:, b * STEP:(b + 1) * STEP]
        attend(query_ref, keys, values, (code > low) & (code < high), acc_ref, total_ref)
    heads = [(acc_ref[h] / total_ref[h][:, :1]).astype(BF16) for h in range(HEADS)]
    attention = jnp.concatenate(heads, axis=1)
    width = out_ref.shape[1]
    for n in range(0, width, 512):
        out_ref[:, n:n + 512] = jnp.dot(
            attention, w_ref[:, n:n + 512], preferred_element_type=F32
        ).astype(BF16)


def far_attention(low, high, query, code, pages, acc, total, w_out):
    vmem = pl.BlockSpec(memory_space=pltpu.VMEM)
    width = w_out.shape[1]
    return pl.pallas_call(
        far_kernel,
        out_shape=jax.ShapeDtypeStruct((128, width), BF16),
        in_specs=[vmem] * 8,
        out_specs=vmem,
        scratch_shapes=[
            pltpu.VMEM((HEADS, 128, HEAD_SIZE), F32),
            pltpu.VMEM((HEADS, 128, 128), F32),
        ],
        cost_estimate=pl.CostEstimate(
            flops=4 * 256 * 2048 * 256, transcendentals=2 * 256 * 2048, bytes_accessed=7_000_000
        ),
        compiler_params=pltpu.CompilerParams(vmem_limit_bytes=24 * 1024 * 1024),
        name="far_attention",
    )(low, high, query, code, pages, acc, total, w_out)


def enter_kernel(own_ref, a_ref, b_ref, c_ref, d_ref, post_ref, ffw_ref, residual_ref, out_ref):
    total = (a_ref[...].astype(F32) + b_ref[...].astype(F32)) + (
        c_ref[...].astype(F32) + d_ref[...].astype(F32)
    )
    residual = own_ref[...].astype(F32) + rms_scale(total, post_ref[...])
    residual_ref[...] = residual
    out_ref[...] = rms_scale(residual, ffw_ref[...]).astype(BF16)


def leave_kernel(residual_ref, a_ref, b_ref, c_ref, d_ref, post_ref, out_ref):
    total = (a_ref[...].astype(F32) + b_ref[...].astype(F32)) + (
        c_ref[...].astype(F32) + d_ref[...].astype(F32)
    )
    out_ref[...] = (residual_ref[...] + rms_scale(total, post_ref[...])).astype(BF16)


def local(
    tokens,
    segment_ids,
    past_len,
    page_table,
    migrate_pages,
    pooled_key_cache,
    pooled_value_cache,
    attn_gain,
    w_query,
    key_matrix,
    value_matrix,
    w_out,
    post_attn_gain,
    ffw_gain,
    w_gate,
    w_up,
    w_down,
    post_ffw_gain,
):
    tok_count, width = tokens.shape
    here = lax.axis_index("mlp")
    other = [(0, 1), (1, 0)]

    packed = pick_pages(migrate_pages.reshape(-1), pooled_key_cache, pooled_value_cache)
    received = lax.all_to_all(packed, REQ, split_axis=0, concat_axis=0, tiled=True)

    gate_sib = lax.ppermute(w_gate, "core", other)
    up_sib = lax.ppermute(w_up, "core", other)
    down_sib = lax.ppermute(w_down, "core", other)

    segment = segment_ids[0]
    past = past_len[0]
    offsets, token_positions = token_layout(segment, past)
    normalized_input = rms_scale(tokens.astype(F32), attn_gain).astype(BF16)
    query_rows = apply_rotary(
        jnp.dot(normalized_input, w_query, preferred_element_type=F32).reshape(
            tok_count, HEADS, HEAD_SIZE
        ),
        token_positions,
    ).astype(BF16)
    incoming_keys = apply_rotary(
        jnp.dot(normalized_input, key_matrix, preferred_element_type=F32).reshape(
            tok_count, 1, HEAD_SIZE
        ),
        token_positions,
    ).astype(BF16).reshape(tok_count, HEAD_SIZE)
    incoming_values = jnp.dot(
        normalized_input, value_matrix, preferred_element_type=F32
    ).astype(BF16)

    page_ids = jnp.arange(2 * POOL, dtype=jnp.int32)
    place = jnp.sum(
        jnp.where(page_table[0][None, :] == page_ids[:, None], page_ids[None, :], 0), axis=1
    )
    page_req = place // WIN_PAGES
    page_past = jnp.sum(
        jnp.where(page_req[:, None] == jnp.arange(4, dtype=jnp.int32)[None, :], past[None, :], 0),
        axis=1,
    )
    slot = (place % WIN_PAGES * PAGE)[:, None] + jnp.arange(PAGE, dtype=jnp.int32)[None, :]
    code = jnp.where(
        slot >= WINDOW_LENGTH - page_past[:, None], page_req[:, None] * 4096 + slot, -1
    ).reshape(1, -1)

    order = (jnp.arange(tok_count, dtype=jnp.int32) + here * ROWS) % tok_count
    turn = lambda v: lax.dynamic_slice_in_dim(jnp.concatenate([v, v], 0), here * ROWS, tok_count, 0)
    low = turn(segment * 4096 + offsets)[:, None]
    high = turn(segment * 4096 + WINDOW_LENGTH)[:, None]
    query = turn(query_rows).transpose(1, 0, 2)
    own_rows = lax.dynamic_slice_in_dim(tokens, here * ROWS, ROWS, 0)

    acc, total = own_attention(
        low, high, order[:, None], segment[None, :], query, incoming_keys, incoming_values,
        code[:, : POOL * PAGE], pooled_key_cache, pooled_value_cache,
    )
    partial = far_attention(
        low, high, query, code[:, POOL * PAGE:], received, acc, total, w_out
    )

    parts = [partial[k * ROWS:(k + 1) * ROWS] for k in range(4)]
    for k in range(1, 4):
        parts[k] = lax.ppermute(parts[k], "mlp", [(i, (i + k) % 4) for i in range(4)])
    vmem = pl.BlockSpec(memory_space=pltpu.VMEM)
    residual, entering = pl.pallas_call(
        enter_kernel,
        out_shape=(
            jax.ShapeDtypeStruct((ROWS, width), F32),
            jax.ShapeDtypeStruct((ROWS, width), BF16),
        ),
        in_specs=[vmem] * 7,
        out_specs=(vmem, vmem),
        name="enter",
    )(own_rows, *parts, post_attn_gain[None, :], ffw_gain[None, :])

    line = jnp.concatenate([entering] + [shift(entering, True, k) for k in (1, 2, 3)], axis=0)
    far = jnp.concatenate([shift(line, False, k) for k in (1, 2, 3)], axis=0)

    def hidden_of(rows, gate, up):
        gate_part = jnp.dot(rows, gate, preferred_element_type=F32)
        up_part = jnp.dot(rows, up, preferred_element_type=F32)
        return (jax.nn.gelu(gate_part, approximate=True) * up_part).astype(BF16)

    def mlp(rows):
        return jnp.dot(hidden_of(rows, w_gate, w_up), w_down, preferred_element_type=F32) + jnp.dot(
            hidden_of(rows, gate_sib, up_sib), down_sib, preferred_element_type=F32
        )

    near_out = mlp(line)
    far_out = mlp(far).astype(BF16)
    step = 4 * ROWS
    back = [shift(far_out[(k - 1) * step:k * step], False, -k) for k in (1, 2, 3)]
    line_out = near_out + sum(b.astype(F32) for b in back)
    line_out = line_out.astype(BF16)
    ends = [line_out[:ROWS]] + [
        shift(line_out[k * ROWS:(k + 1) * ROWS], True, -k) for k in (1, 2, 3)
    ]
    mixed = pl.pallas_call(
        leave_kernel,
        out_shape=jax.ShapeDtypeStruct((ROWS, width), BF16),
        in_specs=[vmem] * 6,
        out_specs=vmem,
        name="leave",
    )(residual, *ends, post_ffw_gain[None, :])
    return (mixed, incoming_keys, incoming_values)


def solution(mesh):
    chips = Mesh(mesh.devices.reshape(4, 4, 2, 4), ("x", "z", "core", "mlp"))
    return jax.shard_map(
        local,
        mesh=chips,
        in_specs=(
            P(REQ, None),
            P(REQ, None),
            P(REQ, None),
            P(REQ, None),
            P(REQ, None, None),
            P(REQ, None, "mlp"),
            P(REQ, None, "mlp"),
            P(),
            P(None, "mlp"),
            P(None, "mlp"),
            P(None, "mlp"),
            P("mlp", None),
            P(),
            P(),
            P(None, REQ),
            P(None, REQ),
            P(REQ, None),
            P(),
        ),
        out_specs=(P((*REQ, "mlp"), None), P(REQ, "mlp"), P(REQ, "mlp")),
        check_vma=False,
    )
```

```python
import jax
import jax.numpy as jnp
from jax import lax
from jax.experimental import pallas as pl
from jax.experimental.pallas import tpu as pltpu
from jax.sharding import Mesh, PartitionSpec as P

HEAD_SIZE = 256
WINDOW_LENGTH = 1024
PAGE = 64
WIN_PAGES = 16
OWNERS = 32
POOL = 32
HEADS = 2
ROWS = 32

SOFT_CAP = 50.0
NORM_EPS = 1e-06
ROPE_BASE = 10000.0

BF16 = jnp.bfloat16
F32 = jnp.float32

REQ = ("x", "z", "core")


def rms_scale(values, gain):
    return values * lax.rsqrt(jnp.mean(values * values, axis=-1, keepdims=True) + NORM_EPS) * gain


def apply_rotary(vectors, token_positions):
    half = HEAD_SIZE // 2
    frequency = ROPE_BASE ** (-jnp.arange(half, dtype=F32) * (2.0 / HEAD_SIZE))
    angles = token_positions.astype(F32)[:, None] * frequency[None, :]
    cosine = jnp.cos(angles)[:, None, :]
    sine = jnp.sin(angles)[:, None, :]
    first = vectors[..., :half]
    second = vectors[..., half:]
    return jnp.concatenate(
        [first * cosine - second * sine, second * cosine + first * sine], axis=-1
    )


def token_layout(segment, past):
    requests = jnp.arange(past.shape[0], dtype=jnp.int32)
    member = segment[:, None] == requests[None, :]
    firsts = jnp.sum((segment[:, None] < requests[None, :]).astype(jnp.int32), axis=0)
    offsets = jnp.arange(segment.shape[0], dtype=jnp.int32) - jnp.sum(
        jnp.where(member, firsts[None, :], 0), axis=1
    )
    token_positions = jnp.sum(jnp.where(member, past[None, :], 0), axis=1) + offsets
    return (offsets, token_positions)


def chip_shift(first, k):
    pairs = []
    for x in range(4):
        for z in range(4):
            for c in range(2):
                if (c == 0) == first:
                    to = ((x + k) % 4, z)
                else:
                    to = (x, (z + k) % 4)
                pairs.append(((x * 4 + z) * 2 + c, (to[0] * 4 + to[1]) * 2 + c))
    return pairs


def shift(value, first, k):
    return lax.ppermute(value, REQ, chip_shift(first, k % 4))


def small(megabytes):
    return pltpu.CompilerParams(vmem_limit_bytes=megabytes * 1024 * 1024)


def pick_pages_kernel(pages_ref, keys_ref, values_ref, out_ref, sems):
    copies = []
    for d in range(OWNERS):
        page = pages_ref[d]
        copies.append(pltpu.make_async_copy(keys_ref.at[page], out_ref.at[d, 0], sems.at[d, 0]))
        copies.append(pltpu.make_async_copy(values_ref.at[page], out_ref.at[d, 1], sems.at[d, 1]))
    for copy in copies:
        copy.start()
    for copy in copies:
        copy.wait()


def pick_pages(pages, keys, values):
    return pl.pallas_call(
        pick_pages_kernel,
        out_shape=jax.ShapeDtypeStruct((OWNERS, 2, PAGE, HEAD_SIZE), BF16),
        grid_spec=pltpu.PrefetchScalarGridSpec(
            num_scalar_prefetch=1,
            grid=(),
            in_specs=[pl.BlockSpec(memory_space=pl.ANY)] * 2,
            out_specs=pl.BlockSpec(memory_space=pltpu.VMEM),
            scratch_shapes=[pltpu.SemaphoreType.DMA((OWNERS, 2))],
        ),
        compiler_params=small(4),
        name="pick_pages",
    )(pages, keys, values)


def weights_of(query, keys, visible):
    scores = lax.dot_general(
        query, keys, (((1,), (1,)), ((), ())), preferred_element_type=F32
    )
    raw = jnp.exp(SOFT_CAP * jnp.tanh(scores * (1.0 / (16.0 * SOFT_CAP))))
    return jnp.where(visible, raw, 0.0)


def attend(query_ref, keys, values, visible, acc_ref, total_ref):
    for h in range(HEADS):
        weight = weights_of(query_ref[h], keys, visible)
        total_ref[h] += jnp.broadcast_to(
            jnp.sum(weight, axis=-1, keepdims=True), total_ref.shape[1:]
        )
        acc_ref[h] += jnp.dot(weight.astype(BF16), values, preferred_element_type=F32)


STEP_PAGES = 8
STEP = STEP_PAGES * PAGE


def own_kernel(low_ref, high_ref, order_ref, seg_row_ref, query_ref, new_keys_ref, new_values_ref,
               code_ref, keys_ref, values_ref, acc_ref, total_ref):
    acc_ref[...] = jnp.zeros_like(acc_ref)
    total_ref[...] = jnp.zeros_like(total_ref)
    low, high, order = low_ref[...], high_ref[...], order_ref[...]
    count = order.shape[0]
    column = lax.broadcasted_iota(jnp.int32, (count, count), 1)
    same = lax.div(high, 4096) == seg_row_ref[...]
    attend(query_ref, new_keys_ref[...], new_values_ref[...], same & (column <= order), acc_ref, total_ref)
    for b in range(POOL // STEP_PAGES):
        keys = keys_ref[b * STEP_PAGES:(b + 1) * STEP_PAGES].reshape(STEP, HEAD_SIZE)
        values = values_ref[b * STEP_PAGES:(b + 1) * STEP_PAGES].reshape(STEP, HEAD_SIZE)
        code = code_ref[:, b * STEP:(b + 1) * STEP]
        attend(query_ref, keys, values, (code > low) & (code < high), acc_ref, total_ref)


def own_attention(low, high, order, seg_row, query, new_keys, new_values, code, keys, values):
    vmem = pl.BlockSpec(memory_space=pltpu.VMEM)
    return pl.pallas_call(
        own_kernel,
        out_shape=(
            jax.ShapeDtypeStruct((HEADS, 128, HEAD_SIZE), F32),
            jax.ShapeDtypeStruct((HEADS, 128, 128), F32),
        ),
        in_specs=[vmem] * 10,
        out_specs=(vmem, vmem),
        cost_estimate=pl.CostEstimate(
            flops=4 * 256 * 2176 * 256, transcendentals=2 * 256 * 2176, bytes_accessed=3_000_000
        ),
        compiler_params=small(10),
        name="own_attention",
    )(low, high, order, seg_row, query, new_keys, new_values, code, keys, values)


def far_kernel(low_ref, high_ref, query_ref, code_ref, pages_ref, acc_in_ref, total_in_ref, w_ref,
               out_ref, acc_ref, total_ref):
    acc_ref[...] = acc_in_ref[...]
    total_ref[...] = total_in_ref[...]
    low, high = low_ref[...], high_ref[...]
    for b in range(OWNERS // STEP_PAGES):
        keys = pages_ref[b * STEP_PAGES:(b + 1) * STEP_PAGES, 0].reshape(STEP, HEAD_SIZE)
        values = pages_ref[b * STEP_PAGES:(b + 1) * STEP_PAGES, 1].reshape(STEP, HEAD_SIZE)
        code = code_ref[:, b * STEP:(b + 1) * STEP]
        attend(query_ref, keys, values, (code > low) & (code < high), acc_ref, total_ref)
    heads = [(acc_ref[h] / total_ref[h][:, :1]).astype(BF16) for h in range(HEADS)]
    attention = jnp.concatenate(heads, axis=1)
    width = out_ref.shape[1]
    for n in range(0, width, 512):
        out_ref[:, n:n + 512] = jnp.dot(
            attention, w_ref[:, n:n + 512], preferred_element_type=F32
        ).astype(BF16)


def far_attention(low, high, query, code, pages, acc, total, w_out):
    vmem = pl.BlockSpec(memory_space=pltpu.VMEM)
    width = w_out.shape[1]
    return pl.pallas_call(
        far_kernel,
        out_shape=jax.ShapeDtypeStruct((128, width), BF16),
        in_specs=[vmem] * 8,
        out_specs=vmem,
        scratch_shapes=[
            pltpu.VMEM((HEADS, 128, HEAD_SIZE), F32),
            pltpu.VMEM((HEADS, 128, 128), F32),
        ],
        cost_estimate=pl.CostEstimate(
            flops=4 * 256 * 2048 * 256, transcendentals=2 * 256 * 2048, bytes_accessed=7_000_000
        ),
        compiler_params=small(12),
        name="far_attention",
    )(low, high, query, code, pages, acc, total, w_out)


def enter_kernel(own_ref, a_ref, b_ref, c_ref, d_ref, post_ref, ffw_ref, residual_ref, out_ref):
    total = (a_ref[...].astype(F32) + b_ref[...].astype(F32)) + (
        c_ref[...].astype(F32) + d_ref[...].astype(F32)
    )
    residual = own_ref[...].astype(F32) + rms_scale(total, post_ref[...])
    residual_ref[...] = residual
    out_ref[...] = rms_scale(residual, ffw_ref[...]).astype(BF16)


def leave_kernel(residual_ref, a_ref, b_ref, c_ref, d_ref, post_ref, out_ref):
    total = (a_ref[...].astype(F32) + b_ref[...].astype(F32)) + (
        c_ref[...].astype(F32) + d_ref[...].astype(F32)
    )
    out_ref[...] = (residual_ref[...] + rms_scale(total, post_ref[...])).astype(BF16)


def mlp_kernel(rows_ref, gate_ref, up_ref, down_ref, gate2_ref, up2_ref, down2_ref, out_ref, hidden_ref):
    rows = rows_ref[...]
    units = gate_ref.shape[0]
    last = (((1,), (1,)), ((), ()))
    for i, (gate, up) in enumerate(((gate_ref, up_ref), (gate2_ref, up2_ref))):
        gate_part = lax.dot_general(rows, gate[...], last, preferred_element_type=F32)
        up_part = lax.dot_general(rows, up[...], last, preferred_element_type=F32)
        hidden_ref[:, i * units:(i + 1) * units] = (
            jax.nn.gelu(gate_part, approximate=True) * up_part
        ).astype(BF16)
    width = out_ref.shape[1]
    for n in range(0, width, 512):
        out_ref[:, n:n + 512] = (
            jnp.dot(hidden_ref[:, :units], down_ref[:, n:n + 512], preferred_element_type=F32)
            + jnp.dot(hidden_ref[:, units:], down2_ref[:, n:n + 512], preferred_element_type=F32)
        ).astype(out_ref.dtype)


def mlp(rows, weights, out_type):
    count, width = rows.shape
    units = weights[0].shape[0]
    vmem = pl.BlockSpec(memory_space=pltpu.VMEM)
    return pl.pallas_call(
        mlp_kernel,
        out_shape=jax.ShapeDtypeStruct((count, width), out_type),
        in_specs=[vmem] * 7,
        out_specs=vmem,
        scratch_shapes=[pltpu.VMEM((count, 2 * units), BF16)],
        cost_estimate=pl.CostEstimate(
            flops=12 * count * width * units,
            transcendentals=2 * count * units,
            bytes_accessed=12 * units * width + 4 * count * width,
        ),
        compiler_params=small(20),
        name="mlp",
    )(rows, *weights)


def local(
    tokens,
    segment_ids,
    past_len,
    page_table,
    migrate_pages,
    pooled_key_cache,
    pooled_value_cache,
    attn_gain,
    w_query,
    key_matrix,
    value_matrix,
    w_out,
    post_attn_gain,
    ffw_gain,
    w_gate,
    w_up,
    w_down,
    post_ffw_gain,
):
    tok_count, width = tokens.shape
    here = lax.axis_index("mlp")
    other = [(0, 1), (1, 0)]

    packed = pick_pages(migrate_pages.reshape(-1), pooled_key_cache, pooled_value_cache)
    received = lax.all_to_all(packed, REQ, split_axis=0, concat_axis=0, tiled=True)

    gate, up = w_gate.T, w_up.T
    weights = (gate, up, w_down) + tuple(
        lax.ppermute(w, "core", other) for w in (gate, up, w_down)
    )

    segment = segment_ids[0]
    past = past_len[0]
    offsets, token_positions = token_layout(segment, past)
    normalized_input = rms_scale(tokens.astype(F32), attn_gain).astype(BF16)
    query_rows = apply_rotary(
        jnp.dot(normalized_input, w_query, preferred_element_type=F32).reshape(
            tok_count, HEADS, HEAD_SIZE
        ),
        token_positions,
    ).astype(BF16)
    incoming_keys = apply_rotary(
        jnp.dot(normalized_input, key_matrix, preferred_element_type=F32).reshape(
            tok_count, 1, HEAD_SIZE
        ),
        token_positions,
    ).astype(BF16).reshape(tok_count, HEAD_SIZE)
    incoming_values = jnp.dot(
        normalized_input, value_matrix, preferred_element_type=F32
    ).astype(BF16)

    page_ids = jnp.arange(2 * POOL, dtype=jnp.int32)
    place = jnp.sum(
        jnp.where(page_table[0][None, :] == page_ids[:, None], page_ids[None, :], 0), axis=1
    )
    page_req = place // WIN_PAGES
    page_past = jnp.sum(
        jnp.where(page_req[:, None] == jnp.arange(4, dtype=jnp.int32)[None, :], past[None, :], 0),
        axis=1,
    )
    slot = (place % WIN_PAGES * PAGE)[:, None] + jnp.arange(PAGE, dtype=jnp.int32)[None, :]
    code = jnp.where(
        slot >= WINDOW_LENGTH - page_past[:, None], page_req[:, None] * 4096 + slot, -1
    ).reshape(1, -1)

    order = (jnp.arange(tok_count, dtype=jnp.int32) + here * ROWS) % tok_count
    turn = lambda v: lax.dynamic_slice_in_dim(jnp.concatenate([v, v], 0), here * ROWS, tok_count, 0)
    low = turn(segment * 4096 + offsets)[:, None]
    high = turn(segment * 4096 + WINDOW_LENGTH)[:, None]
    query = turn(query_rows).transpose(1, 0, 2)
    own_rows = lax.dynamic_slice_in_dim(tokens, here * ROWS, ROWS, 0)

    acc, total = own_attention(
        low, high, order[:, None], segment[None, :], query, incoming_keys, incoming_values,
        code[:, : POOL * PAGE], pooled_key_cache, pooled_value_cache,
    )
    partial = far_attention(
        low, high, query, code[:, POOL * PAGE:], received, acc, total, w_out
    )

    parts = [partial[k * ROWS:(k + 1) * ROWS] for k in range(4)]
    for k in range(1, 4):
        parts[k] = lax.ppermute(parts[k], "mlp", [(i, (i + k) % 4) for i in range(4)])
    vmem = pl.BlockSpec(memory_space=pltpu.VMEM)
    residual, entering = pl.pallas_call(
        enter_kernel,
        out_shape=(
            jax.ShapeDtypeStruct((ROWS, width), F32),
            jax.ShapeDtypeStruct((ROWS, width), BF16),
        ),
        in_specs=[vmem] * 7,
        out_specs=(vmem, vmem),
        compiler_params=small(6),
        name="enter",
    )(own_rows, *parts, post_attn_gain[None, :], ffw_gain[None, :])

    line = jnp.concatenate([entering] + [shift(entering, True, k) for k in (1, 2, 3)], axis=0)
    near_out = mlp(line, weights, F32)
    sides = jnp.concatenate([shift(line, False, k) for k in (1, 3)], axis=0)
    line_later, near_out = lax.optimization_barrier((line, near_out))
    across = shift(line_later, False, 2)
    side_out = mlp(sides, weights, BF16)
    across_out = mlp(across, weights, BF16)
    step = 4 * ROWS
    back = [shift(side_out[:step], False, -1), shift(side_out[step:], False, -3), shift(across_out, False, -2)]
    line_out = near_out + sum(b.astype(F32) for b in back)
    line_out = line_out.astype(BF16)
    ends = [line_out[:ROWS]] + [
        shift(line_out[k * ROWS:(k + 1) * ROWS], True, -k) for k in (1, 2, 3)
    ]
    mixed = pl.pallas_call(
        leave_kernel,
        out_shape=jax.ShapeDtypeStruct((ROWS, width), BF16),
        in_specs=[vmem] * 6,
        out_specs=vmem,
        compiler_params=small(6),
        name="leave",
    )(residual, *ends, post_ffw_gain[None, :])
    return (mixed, incoming_keys, incoming_values)


def solution(mesh):
    chips = Mesh(mesh.devices.reshape(4, 4, 2, 4), ("x", "z", "core", "mlp"))
    return jax.shard_map(
        local,
        mesh=chips,
        in_specs=(
            P(REQ, None),
            P(REQ, None),
            P(REQ, None),
            P(REQ, None),
            P(REQ, None, None),
            P(REQ, None, "mlp"),
            P(REQ, None, "mlp"),
            P(),
            P(None, "mlp"),
            P(None, "mlp"),
            P(None, "mlp"),
            P("mlp", None),
            P(),
            P(),
            P(None, REQ),
            P(None, REQ),
            P(REQ, None),
            P(),
        ),
        out_specs=(P((*REQ, "mlp"), None), P(REQ, "mlp"), P(REQ, "mlp")),
        check_vma=False,
    )
```

```python
import jax
import jax.numpy as jnp
from jax import lax
from jax.experimental import pallas as pl
from jax.experimental.pallas import tpu as pltpu
from jax.sharding import Mesh, PartitionSpec as P

HEAD_SIZE = 256
WINDOW_LENGTH = 1024
PAGE = 64
WIN_PAGES = 16
OWNERS = 32
POOL = 32
HEADS = 2
ROWS = 32

SOFT_CAP = 50.0
NORM_EPS = 1e-06
ROPE_BASE = 10000.0
MLP_MIB = 8
LOAD_MIB = 40
FAR_MIB = 58

BF16 = jnp.bfloat16
F32 = jnp.float32

REQ = ("x", "z", "core")


def rms_scale(values, gain):
    return values * lax.rsqrt(jnp.mean(values * values, axis=-1, keepdims=True) + NORM_EPS) * gain


def apply_rotary(vectors, token_positions):
    half = HEAD_SIZE // 2
    frequency = ROPE_BASE ** (-jnp.arange(half, dtype=F32) * (2.0 / HEAD_SIZE))
    angles = token_positions.astype(F32)[:, None] * frequency[None, :]
    cosine = jnp.cos(angles)[:, None, :]
    sine = jnp.sin(angles)[:, None, :]
    first = vectors[..., :half]
    second = vectors[..., half:]
    return jnp.concatenate(
        [first * cosine - second * sine, second * cosine + first * sine], axis=-1
    )


def token_layout(segment, past):
    requests = jnp.arange(past.shape[0], dtype=jnp.int32)
    member = segment[:, None] == requests[None, :]
    firsts = jnp.sum((segment[:, None] < requests[None, :]).astype(jnp.int32), axis=0)
    offsets = jnp.arange(segment.shape[0], dtype=jnp.int32) - jnp.sum(
        jnp.where(member, firsts[None, :], 0), axis=1
    )
    token_positions = jnp.sum(jnp.where(member, past[None, :], 0), axis=1) + offsets
    return (offsets, token_positions)


def chip_shift(first, k):
    pairs = []
    for x in range(4):
        for z in range(4):
            for c in range(2):
                if (c == 0) == first:
                    to = ((x + k) % 4, z)
                else:
                    to = (x, (z + k) % 4)
                pairs.append(((x * 4 + z) * 2 + c, (to[0] * 4 + to[1]) * 2 + c))
    return pairs


def shift(value, first, k):
    return lax.ppermute(value, REQ, chip_shift(first, k % 4))


def small(megabytes):
    return pltpu.CompilerParams(vmem_limit_bytes=megabytes * 1024 * 1024)


def pick_pages_kernel(pages_ref, keys_ref, values_ref, out_ref, held_ref, in_sems, out_sems):
    loads = []
    for d in range(OWNERS):
        page = pages_ref[d]
        loads.append((
            pltpu.make_async_copy(keys_ref.at[page], held_ref.at[d, 0], in_sems.at[d, 0]),
            pltpu.make_async_copy(values_ref.at[page], held_ref.at[d, 1], in_sems.at[d, 1]),
        ))
        for load in loads[d]:
            load.start()
    stores = []
    for d in range(0, OWNERS, 4):
        for e in range(d, d + 4):
            for load in loads[e]:
                load.wait()
        stores.append(
            pltpu.make_async_copy(held_ref.at[d:d + 4], out_ref.at[d:d + 4], out_sems.at[d // 4])
        )
        stores[-1].start()
    for store in stores:
        store.wait()


def pick_pages(pages, keys, values):
    hbm = pl.BlockSpec(memory_space=pltpu.HBM)
    return pl.pallas_call(
        pick_pages_kernel,
        out_shape=jax.ShapeDtypeStruct((OWNERS, 2, PAGE, HEAD_SIZE), BF16),
        grid_spec=pltpu.PrefetchScalarGridSpec(
            num_scalar_prefetch=1,
            grid=(),
            in_specs=[hbm] * 2,
            out_specs=hbm,
            scratch_shapes=[
                pltpu.VMEM((OWNERS, 2, PAGE, HEAD_SIZE), BF16),
                pltpu.SemaphoreType.DMA((OWNERS, 2)),
                pltpu.SemaphoreType.DMA((OWNERS // 4,)),
            ],
        ),
        compiler_params=small(56),
        name="pick_pages",
    )(pages, keys, values)


def load_kernel(*refs):
    *weights, out_ref, sems = refs
    copies = [
        pltpu.make_async_copy(w, out_ref.at[i], sems.at[i]) for i, w in enumerate(weights)
    ]
    for copy in copies:
        copy.start()
    for copy in copies:
        copy.wait()


def load_weights(weights):
    units, width = weights[0].shape
    count = len(weights)
    return pl.pallas_call(
        load_kernel,
        out_shape=pltpu.VMEM((count, units, width), BF16),
        in_specs=[pl.BlockSpec(memory_space=pltpu.HBM)] * count,
        out_specs=pl.BlockSpec(memory_space=pltpu.VMEM),
        scratch_shapes=[pltpu.SemaphoreType.DMA((count,))],
        cost_estimate=pl.CostEstimate(
            flops=0, transcendentals=0, bytes_accessed=2 * count * units * width
        ),
        compiler_params=small(LOAD_MIB),
        name="load_weights",
    )(*weights)


def weights_of(query, keys, visible):
    scores = lax.dot_general(
        query, keys, (((1,), (1,)), ((), ())), preferred_element_type=F32
    )
    raw = jnp.exp(SOFT_CAP * jnp.tanh(scores * (1.0 / (16.0 * SOFT_CAP))))
    return jnp.where(visible, raw, 0.0)


def attend(query_ref, keys, values, visible, acc_ref, total_ref):
    for h in range(HEADS):
        weight = weights_of(query_ref[h], keys, visible)
        total_ref[h] += jnp.broadcast_to(
            jnp.sum(weight, axis=-1, keepdims=True), total_ref.shape[1:]
        )
        acc_ref[h] += jnp.dot(weight.astype(BF16), values, preferred_element_type=F32)


STEP_PAGES = 8
STEP = STEP_PAGES * PAGE


def own_kernel(low_ref, high_ref, order_ref, seg_row_ref, query_ref, new_keys_ref, new_values_ref,
               code_ref, keys_ref, values_ref, acc_ref, total_ref):
    acc_ref[...] = jnp.zeros_like(acc_ref)
    total_ref[...] = jnp.zeros_like(total_ref)
    low, high, order = low_ref[...], high_ref[...], order_ref[...]
    count = order.shape[0]
    column = lax.broadcasted_iota(jnp.int32, (count, count), 1)
    same = lax.div(high, 4096) == seg_row_ref[...]
    attend(query_ref, new_keys_ref[...], new_values_ref[...], same & (column <= order), acc_ref, total_ref)
    for b in range(POOL // STEP_PAGES):
        keys = keys_ref[b * STEP_PAGES:(b + 1) * STEP_PAGES].reshape(STEP, HEAD_SIZE)
        values = values_ref[b * STEP_PAGES:(b + 1) * STEP_PAGES].reshape(STEP, HEAD_SIZE)
        code = code_ref[:, b * STEP:(b + 1) * STEP]
        attend(query_ref, keys, values, (code > low) & (code < high), acc_ref, total_ref)


def own_attention(low, high, order, seg_row, query, new_keys, new_values, code, keys, values):
    vmem = pl.BlockSpec(memory_space=pltpu.VMEM)
    return pl.pallas_call(
        own_kernel,
        out_shape=(
            jax.ShapeDtypeStruct((HEADS, 128, HEAD_SIZE), F32),
            jax.ShapeDtypeStruct((HEADS, 128, 128), F32),
        ),
        in_specs=[vmem] * 10,
        out_specs=(vmem, vmem),
        cost_estimate=pl.CostEstimate(
            flops=4 * 256 * 2176 * 256, transcendentals=2 * 256 * 2176, bytes_accessed=3_000_000
        ),
        compiler_params=small(10),
        name="own_attention",
    )(low, high, order, seg_row, query, new_keys, new_values, code, keys, values)


def far_kernel(low_ref, high_ref, query_ref, code_ref, acc_in_ref, total_in_ref, pages_ref, w_ref,
               out_ref, acc_ref, total_ref, held_ref, w_held_ref, page_sems, w_sem):
    loads = [
        pltpu.make_async_copy(
            pages_ref.at[b * STEP_PAGES:(b + 1) * STEP_PAGES], held_ref.at[b], page_sems.at[b]
        )
        for b in range(OWNERS // STEP_PAGES)
    ]
    for load in loads:
        load.start()
    w_load = pltpu.make_async_copy(w_ref, w_held_ref, w_sem)
    w_load.start()
    acc_ref[...] = acc_in_ref[...]
    total_ref[...] = total_in_ref[...]
    low, high = low_ref[...], high_ref[...]
    for b in range(OWNERS // STEP_PAGES):
        loads[b].wait()
        keys = held_ref[b, :, 0].reshape(STEP, HEAD_SIZE)
        values = held_ref[b, :, 1].reshape(STEP, HEAD_SIZE)
        code = code_ref[:, b * STEP:(b + 1) * STEP]
        attend(query_ref, keys, values, (code > low) & (code < high), acc_ref, total_ref)
    heads = [(acc_ref[h] / total_ref[h][:, :1]).astype(BF16) for h in range(HEADS)]
    attention = jnp.concatenate(heads, axis=1)
    width = out_ref.shape[1]
    w_load.wait()
    for n in range(0, width, 512):
        out_ref[:, n:n + 512] = jnp.dot(
            attention, w_held_ref[:, n:n + 512], preferred_element_type=F32
        ).astype(BF16)


def far_attention(low, high, query, code, acc, total, pages, w_out):
    vmem = pl.BlockSpec(memory_space=pltpu.VMEM)
    hbm = pl.BlockSpec(memory_space=pltpu.HBM)
    width = w_out.shape[1]
    return pl.pallas_call(
        far_kernel,
        out_shape=jax.ShapeDtypeStruct((128, width), BF16),
        in_specs=[vmem] * 6 + [hbm] * 2,
        out_specs=vmem,
        scratch_shapes=[
            pltpu.VMEM((HEADS, 128, HEAD_SIZE), F32),
            pltpu.VMEM((HEADS, 128, 128), F32),
            pltpu.VMEM((OWNERS // STEP_PAGES, STEP_PAGES, 2, PAGE, HEAD_SIZE), BF16),
            pltpu.VMEM(w_out.shape, BF16),
            pltpu.SemaphoreType.DMA((OWNERS // STEP_PAGES,)),
            pltpu.SemaphoreType.DMA,
        ],
        cost_estimate=pl.CostEstimate(
            flops=4 * 256 * 2048 * 256, transcendentals=2 * 256 * 2048, bytes_accessed=7_000_000
        ),
        compiler_params=small(FAR_MIB),
        name="far_attention",
    )(low, high, query, code, acc, total, pages, w_out)


def enter_kernel(own_ref, a_ref, b_ref, c_ref, d_ref, post_ref, ffw_ref, residual_ref, out_ref):
    total = (a_ref[...].astype(F32) + b_ref[...].astype(F32)) + (
        c_ref[...].astype(F32) + d_ref[...].astype(F32)
    )
    residual = own_ref[...].astype(F32) + rms_scale(total, post_ref[...])
    residual_ref[...] = residual
    out_ref[...] = rms_scale(residual, ffw_ref[...]).astype(BF16)


def leave_kernel(residual_ref, a_ref, b_ref, c_ref, d_ref, post_ref, out_ref):
    total = (a_ref[...].astype(F32) + b_ref[...].astype(F32)) + (
        c_ref[...].astype(F32) + d_ref[...].astype(F32)
    )
    out_ref[...] = (residual_ref[...] + rms_scale(total, post_ref[...])).astype(BF16)


def mlp_kernel(rows_ref, weights_ref, out_ref, hidden_ref):
    rows = rows_ref[...]
    units = weights_ref.shape[1]
    last = (((1,), (1,)), ((), ()))
    for i in range(2):
        gate_part = lax.dot_general(rows, weights_ref[3 * i], last, preferred_element_type=F32)
        up_part = lax.dot_general(rows, weights_ref[3 * i + 1], last, preferred_element_type=F32)
        hidden_ref[:, i * units:(i + 1) * units] = (
            jax.nn.gelu(gate_part, approximate=True) * up_part
        ).astype(BF16)
    width = out_ref.shape[1]
    for n in range(0, width, 512):
        total = jnp.dot(
            hidden_ref[:, :units], weights_ref[2, :, n:n + 512], preferred_element_type=F32
        ) + jnp.dot(
            hidden_ref[:, units:], weights_ref[5, :, n:n + 512], preferred_element_type=F32
        )
        out_ref[:, n:n + 512] = total.astype(out_ref.dtype)


def mlp(rows, weights, out_type):
    count, width = rows.shape
    units = weights.shape[1]
    vmem = pl.BlockSpec(memory_space=pltpu.VMEM)
    return pl.pallas_call(
        mlp_kernel,
        out_shape=jax.ShapeDtypeStruct((count, width), out_type),
        in_specs=[vmem] * 2,
        out_specs=vmem,
        scratch_shapes=[pltpu.VMEM((count, 2 * units), BF16)],
        cost_estimate=pl.CostEstimate(
            flops=12 * count * width * units,
            transcendentals=2 * count * units,
            bytes_accessed=4 * count * width,
        ),
        compiler_params=small(MLP_MIB),
        name="mlp",
    )(rows, weights)


def local(
    tokens,
    segment_ids,
    past_len,
    page_table,
    migrate_pages,
    pooled_key_cache,
    pooled_value_cache,
    attn_gain,
    w_query,
    key_matrix,
    value_matrix,
    w_out,
    post_attn_gain,
    ffw_gain,
    w_gate,
    w_up,
    w_down,
    post_ffw_gain,
):
    tok_count, width = tokens.shape
    here = lax.axis_index("mlp")
    other = [(0, 1), (1, 0)]

    packed = pick_pages(migrate_pages.reshape(-1), pooled_key_cache, pooled_value_cache)
    received = lax.all_to_all(packed, REQ, split_axis=0, concat_axis=0, tiled=True)

    gate, up = w_gate.T, w_up.T
    weights = (gate, up, w_down) + tuple(
        lax.ppermute(w, "core", other) for w in (gate, up, w_down)
    )

    segment = segment_ids[0]
    past = past_len[0]
    offsets, token_positions = token_layout(segment, past)
    normalized_input = rms_scale(tokens.astype(F32), attn_gain).astype(BF16)
    query_rows = apply_rotary(
        jnp.dot(normalized_input, w_query, preferred_element_type=F32).reshape(
            tok_count, HEADS, HEAD_SIZE
        ),
        token_positions,
    ).astype(BF16)
    incoming_keys = apply_rotary(
        jnp.dot(normalized_input, key_matrix, preferred_element_type=F32).reshape(
            tok_count, 1, HEAD_SIZE
        ),
        token_positions,
    ).astype(BF16).reshape(tok_count, HEAD_SIZE)
    incoming_values = jnp.dot(
        normalized_input, value_matrix, preferred_element_type=F32
    ).astype(BF16)

    page_ids = jnp.arange(2 * POOL, dtype=jnp.int32)
    place = jnp.sum(
        jnp.where(page_table[0][None, :] == page_ids[:, None], page_ids[None, :], 0), axis=1
    )
    page_req = place // WIN_PAGES
    page_past = jnp.sum(
        jnp.where(page_req[:, None] == jnp.arange(4, dtype=jnp.int32)[None, :], past[None, :], 0),
        axis=1,
    )
    slot = (place % WIN_PAGES * PAGE)[:, None] + jnp.arange(PAGE, dtype=jnp.int32)[None, :]
    code = jnp.where(
        slot >= WINDOW_LENGTH - page_past[:, None], page_req[:, None] * 4096 + slot, -1
    ).reshape(1, -1)

    order = (jnp.arange(tok_count, dtype=jnp.int32) + here * ROWS) % tok_count
    turn = lambda v: lax.dynamic_slice_in_dim(jnp.concatenate([v, v], 0), here * ROWS, tok_count, 0)
    low = turn(segment * 4096 + offsets)[:, None]
    high = turn(segment * 4096 + WINDOW_LENGTH)[:, None]
    query = turn(query_rows).transpose(1, 0, 2)
    own_rows = lax.dynamic_slice_in_dim(tokens, here * ROWS, ROWS, 0)

    acc, total = own_attention(
        low, high, order[:, None], segment[None, :], query, incoming_keys, incoming_values,
        code[:, : POOL * PAGE], pooled_key_cache, pooled_value_cache,
    )
    partial = far_attention(
        low, high, query, code[:, POOL * PAGE:], acc, total, received, w_out
    )

    weights, partial = lax.optimization_barrier((weights, partial))
    weights = load_weights(weights)
    parts = [partial[k * ROWS:(k + 1) * ROWS] for k in range(4)]
    for k in range(1, 4):
        parts[k] = lax.ppermute(parts[k], "mlp", [(i, (i + k) % 4) for i in range(4)])
    vmem = pl.BlockSpec(memory_space=pltpu.VMEM)
    residual, entering = pl.pallas_call(
        enter_kernel,
        out_shape=(
            jax.ShapeDtypeStruct((ROWS, width), F32),
            jax.ShapeDtypeStruct((ROWS, width), BF16),
        ),
        in_specs=[vmem] * 7,
        out_specs=(vmem, vmem),
        compiler_params=small(6),
        name="enter",
    )(own_rows, *parts, post_attn_gain[None, :], ffw_gain[None, :])

    line = jnp.concatenate([entering] + [shift(entering, True, k) for k in (1, 2, 3)], axis=0)
    near_out = mlp(line, weights, F32)
    sides = jnp.concatenate([shift(line, False, k) for k in (1, 3)], axis=0)
    across = shift(line, False, 2)
    side_out = mlp(sides, weights, BF16)
    across_out = mlp(across, weights, BF16)
    step = 4 * ROWS
    back = [shift(side_out[:step], False, -1), shift(side_out[step:], False, -3), shift(across_out, False, -2)]
    line_out = near_out + sum(b.astype(F32) for b in back)
    line_out = line_out.astype(BF16)
    ends = [line_out[:ROWS]] + [
        shift(line_out[k * ROWS:(k + 1) * ROWS], True, -k) for k in (1, 2, 3)
    ]
    mixed = pl.pallas_call(
        leave_kernel,
        out_shape=jax.ShapeDtypeStruct((ROWS, width), BF16),
        in_specs=[vmem] * 6,
        out_specs=vmem,
        compiler_params=small(6),
        name="leave",
    )(residual, *ends, post_ffw_gain[None, :])
    return (mixed, incoming_keys, incoming_values)


def solution(mesh):
    chips = Mesh(mesh.devices.reshape(4, 4, 2, 4), ("x", "z", "core", "mlp"))
    return jax.shard_map(
        local,
        mesh=chips,
        in_specs=(
            P(REQ, None),
            P(REQ, None),
            P(REQ, None),
            P(REQ, None),
            P(REQ, None, None),
            P(REQ, None, "mlp"),
            P(REQ, None, "mlp"),
            P(),
            P(None, "mlp"),
            P(None, "mlp"),
            P(None, "mlp"),
            P("mlp", None),
            P(),
            P(),
            P(None, REQ),
            P(None, REQ),
            P(REQ, None),
            P(),
        ),
        out_specs=(P((*REQ, "mlp"), None), P(REQ, "mlp"), P(REQ, "mlp")),
        check_vma=False,
    )
```

```python
import jax
import jax.numpy as jnp
from jax import lax
from jax.experimental import pallas as pl
from jax.experimental.pallas import tpu as pltpu
from jax.sharding import Mesh, PartitionSpec as P

HEAD_SIZE = 256
WINDOW_LENGTH = 1024
PAGE = 64
WIN_PAGES = 16
OWNERS = 32
POOL = 32
HEADS = 2
ROWS = 32

SOFT_CAP = 50.0
NORM_EPS = 1e-06
ROPE_BASE = 10000.0
MLP_MIB = 8
LOAD_MIB = 4
FAR_MIB = 58

BF16 = jnp.bfloat16
F32 = jnp.float32

REQ = ("x", "z", "core")


def rms_scale(values, gain):
    return values * lax.rsqrt(jnp.mean(values * values, axis=-1, keepdims=True) + NORM_EPS) * gain


def apply_rotary(vectors, token_positions):
    half = HEAD_SIZE // 2
    frequency = ROPE_BASE ** (-jnp.arange(half, dtype=F32) * (2.0 / HEAD_SIZE))
    angles = token_positions.astype(F32)[:, None] * frequency[None, :]
    cosine = jnp.cos(angles)[:, None, :]
    sine = jnp.sin(angles)[:, None, :]
    first = vectors[..., :half]
    second = vectors[..., half:]
    return jnp.concatenate(
        [first * cosine - second * sine, second * cosine + first * sine], axis=-1
    )


def token_layout(segment, past):
    requests = jnp.arange(past.shape[0], dtype=jnp.int32)
    member = segment[:, None] == requests[None, :]
    firsts = jnp.sum((segment[:, None] < requests[None, :]).astype(jnp.int32), axis=0)
    offsets = jnp.arange(segment.shape[0], dtype=jnp.int32) - jnp.sum(
        jnp.where(member, firsts[None, :], 0), axis=1
    )
    token_positions = jnp.sum(jnp.where(member, past[None, :], 0), axis=1) + offsets
    return (offsets, token_positions)


def chip_shift(first, k):
    pairs = []
    for x in range(4):
        for z in range(4):
            for c in range(2):
                if (c == 0) == first:
                    to = ((x + k) % 4, z)
                else:
                    to = (x, (z + k) % 4)
                pairs.append(((x * 4 + z) * 2 + c, (to[0] * 4 + to[1]) * 2 + c))
    return pairs


def shift(value, first, k):
    return lax.ppermute(value, REQ, chip_shift(first, k % 4))


def small(megabytes):
    return pltpu.CompilerParams(vmem_limit_bytes=megabytes * 1024 * 1024)


GROUP = 8


def pick_pages_kernel(pages_ref, keys_ref, values_ref, out_ref, keys_held, values_held, held_ref,
                      in_sems, out_sems):
    loads = []
    for g in range(POOL // GROUP):
        part = pl.ds(g * GROUP, GROUP)
        loads.append(pltpu.make_async_copy(keys_ref.at[part], keys_held.at[part], in_sems.at[0, g]))
        loads.append(pltpu.make_async_copy(values_ref.at[part], values_held.at[part], in_sems.at[1, g]))
    for load in loads:
        load.start()
    for load in loads:
        load.wait()
    stores = []
    for g in range(OWNERS // GROUP):
        for d in range(g * GROUP, (g + 1) * GROUP):
            page = pages_ref[d]
            held_ref[d, 0] = keys_held[page]
            held_ref[d, 1] = values_held[page]
        part = pl.ds(g * GROUP, GROUP)
        stores.append(pltpu.make_async_copy(held_ref.at[part], out_ref.at[part], out_sems.at[g]))
        stores[-1].start()
    for store in stores:
        store.wait()


def pick_pages(pages, keys, values):
    hbm = pl.BlockSpec(memory_space=pltpu.HBM)
    return pl.pallas_call(
        pick_pages_kernel,
        out_shape=jax.ShapeDtypeStruct((OWNERS, 2, PAGE, HEAD_SIZE), BF16),
        grid_spec=pltpu.PrefetchScalarGridSpec(
            num_scalar_prefetch=1,
            grid=(),
            in_specs=[hbm] * 2,
            out_specs=hbm,
            scratch_shapes=[
                pltpu.VMEM((POOL, PAGE, HEAD_SIZE), BF16),
                pltpu.VMEM((POOL, PAGE, HEAD_SIZE), BF16),
                pltpu.VMEM((OWNERS, 2, PAGE, HEAD_SIZE), BF16),
                pltpu.SemaphoreType.DMA((2, POOL // GROUP)),
                pltpu.SemaphoreType.DMA((OWNERS // GROUP,)),
            ],
        ),
        compiler_params=small(56),
        name="pick_pages",
    )(pages, keys, values)


def load_kernel(*refs):
    *weights, out_ref, sems = refs
    copies = [
        pltpu.make_async_copy(w, out_ref.at[i], sems.at[i]) for i, w in enumerate(weights)
    ]
    for copy in copies:
        copy.start()
    for copy in copies:
        copy.wait()


def load_weights(weights):
    units, width = weights[0].shape
    count = len(weights)
    return pl.pallas_call(
        load_kernel,
        out_shape=pltpu.VMEM((count, units, width), BF16),
        in_specs=[pl.BlockSpec(memory_space=pltpu.HBM)] * count,
        out_specs=pl.BlockSpec(memory_space=pltpu.VMEM),
        scratch_shapes=[pltpu.SemaphoreType.DMA((count,))],
        cost_estimate=pl.CostEstimate(
            flops=0, transcendentals=0, bytes_accessed=2 * count * units * width
        ),
        compiler_params=small(LOAD_MIB),
        name="load_weights",
    )(*weights)


def weights_of(query, keys, visible):
    scores = lax.dot_general(
        query, keys, (((1,), (1,)), ((), ())), preferred_element_type=F32
    )
    raw = jnp.exp(SOFT_CAP * jnp.tanh(scores * (1.0 / (16.0 * SOFT_CAP))))
    return jnp.where(visible, raw, 0.0)


def attend(query_ref, keys, values, visible, acc_ref, total_ref):
    for h in range(HEADS):
        weight = weights_of(query_ref[h], keys, visible)
        total_ref[h] += jnp.broadcast_to(
            jnp.sum(weight, axis=-1, keepdims=True), total_ref.shape[1:]
        )
        acc_ref[h] += jnp.dot(weight.astype(BF16), values, preferred_element_type=F32)


STEP_PAGES = 8
STEP = STEP_PAGES * PAGE


def own_kernel(low_ref, high_ref, order_ref, seg_row_ref, query_ref, new_keys_ref, new_values_ref,
               code_ref, keys_ref, values_ref, acc_ref, total_ref):
    acc_ref[...] = jnp.zeros_like(acc_ref)
    total_ref[...] = jnp.zeros_like(total_ref)
    low, high, order = low_ref[...], high_ref[...], order_ref[...]
    count = order.shape[0]
    column = lax.broadcasted_iota(jnp.int32, (count, count), 1)
    same = lax.div(high, 4096) == seg_row_ref[...]
    attend(query_ref, new_keys_ref[...], new_values_ref[...], same & (column <= order), acc_ref, total_ref)
    for b in range(POOL // STEP_PAGES):
        keys = keys_ref[b * STEP_PAGES:(b + 1) * STEP_PAGES].reshape(STEP, HEAD_SIZE)
        values = values_ref[b * STEP_PAGES:(b + 1) * STEP_PAGES].reshape(STEP, HEAD_SIZE)
        code = code_ref[:, b * STEP:(b + 1) * STEP]
        attend(query_ref, keys, values, (code > low) & (code < high), acc_ref, total_ref)


def own_attention(low, high, order, seg_row, query, new_keys, new_values, code, keys, values):
    vmem = pl.BlockSpec(memory_space=pltpu.VMEM)
    return pl.pallas_call(
        own_kernel,
        out_shape=(
            jax.ShapeDtypeStruct((HEADS, 128, HEAD_SIZE), F32),
            jax.ShapeDtypeStruct((HEADS, 128, 128), F32),
        ),
        in_specs=[vmem] * 10,
        out_specs=(vmem, vmem),
        cost_estimate=pl.CostEstimate(
            flops=4 * 256 * 2176 * 256, transcendentals=2 * 256 * 2176, bytes_accessed=3_000_000
        ),
        compiler_params=small(10),
        name="own_attention",
    )(low, high, order, seg_row, query, new_keys, new_values, code, keys, values)


def far_kernel(low_hbm, high_hbm, code_hbm, query_hbm, acc_hbm, total_hbm, pages_ref, w_hbm, *refs):
    (*out_refs, acc_ref, total_ref, query_ref, acc_in_ref, total_in_ref, held_ref, w_ref,
     low_ref, high_ref, code_ref, page_sems, sems) = refs
    blocks = OWNERS // STEP_PAGES
    loads = [
        pltpu.make_async_copy(
            pages_ref.at[b * STEP_PAGES:(b + 1) * STEP_PAGES], held_ref.at[b], page_sems.at[b]
        )
        for b in range(blocks)
    ]
    query_load = pltpu.make_async_copy(query_hbm, query_ref, sems.at[0])
    acc_load = pltpu.make_async_copy(acc_hbm, acc_in_ref, sems.at[1])
    total_load = pltpu.make_async_copy(total_hbm, total_in_ref, sems.at[2])
    w_load = pltpu.make_async_copy(w_hbm, w_ref, sems.at[3])
    small_loads = [
        pltpu.make_async_copy(low_hbm, low_ref, sems.at[4]),
        pltpu.make_async_copy(high_hbm, high_ref, sems.at[5]),
        pltpu.make_async_copy(code_hbm, code_ref, sems.at[6]),
        query_load,
    ]
    for load in small_loads:
        load.start()
    for load in loads:
        load.start()
    acc_ref[...] = jnp.zeros_like(acc_ref)
    total_ref[...] = jnp.zeros_like(total_ref)
    for load in small_loads:
        load.wait()
    low, high = low_ref[...], high_ref[...]
    for b in range(blocks):
        loads[b].wait()
        if b == 0:
            w_load.start()
            acc_load.start()
            total_load.start()
        keys = held_ref[b, :, 0].reshape(STEP, HEAD_SIZE)
        values = held_ref[b, :, 1].reshape(STEP, HEAD_SIZE)
        code = code_ref[:, b * STEP:(b + 1) * STEP]
        attend(query_ref, keys, values, (code > low) & (code < high), acc_ref, total_ref)
    acc_load.wait()
    total_load.wait()
    heads = [
        ((acc_ref[h] + acc_in_ref[h]) / (total_ref[h] + total_in_ref[h])[:, :1]).astype(BF16)
        for h in range(HEADS)
    ]
    attention = jnp.concatenate(heads, axis=1)
    rows, width = out_refs[0].shape
    w_load.wait()
    for n in range(0, width, 512):
        block = jnp.dot(
            attention, w_ref[:, n:n + 512], preferred_element_type=F32
        ).astype(BF16)
        for i, out_ref in enumerate(out_refs):
            out_ref[:, n:n + 512] = block[i * rows:(i + 1) * rows]


def far_attention(low, high, query, code, acc, total, pages, w_out, blocks):
    vmem = pl.BlockSpec(memory_space=pltpu.VMEM)
    hbm = pl.BlockSpec(memory_space=pltpu.HBM)
    width = w_out.shape[1]
    return pl.pallas_call(
        far_kernel,
        out_shape=[pltpu.VMEM((128 // blocks, width), BF16)] * blocks,
        in_specs=[hbm] * 8,
        out_specs=[vmem] * blocks,
        scratch_shapes=[
            pltpu.VMEM((HEADS, 128, HEAD_SIZE), F32),
            pltpu.VMEM((HEADS, 128, 128), F32),
            pltpu.VMEM((HEADS, 128, HEAD_SIZE), BF16),
            pltpu.VMEM((HEADS, 128, HEAD_SIZE), F32),
            pltpu.VMEM((HEADS, 128, 128), F32),
            pltpu.VMEM((OWNERS // STEP_PAGES, STEP_PAGES, 2, PAGE, HEAD_SIZE), BF16),
            pltpu.VMEM(w_out.shape, BF16),
            pltpu.VMEM(low.shape, jnp.int32),
            pltpu.VMEM(high.shape, jnp.int32),
            pltpu.VMEM(code.shape, jnp.int32),
            pltpu.SemaphoreType.DMA((OWNERS // STEP_PAGES,)),
            pltpu.SemaphoreType.DMA((7,)),
        ],
        cost_estimate=pl.CostEstimate(
            flops=4 * 256 * 2048 * 256, transcendentals=2 * 256 * 2048, bytes_accessed=7_000_000
        ),
        compiler_params=small(FAR_MIB),
        name="far_attention",
    )(low, high, code, query, acc, total, pages, w_out)


def enter_kernel(own_ref, a_ref, b_ref, c_ref, d_ref, post_ref, ffw_ref, residual_ref, out_ref):
    total = (a_ref[...].astype(F32) + b_ref[...].astype(F32)) + (
        c_ref[...].astype(F32) + d_ref[...].astype(F32)
    )
    residual = own_ref[...].astype(F32) + rms_scale(total, post_ref[...])
    residual_ref[...] = residual
    out_ref[...] = rms_scale(residual, ffw_ref[...]).astype(BF16)


def leave_kernel(residual_ref, a_ref, b_ref, c_ref, d_ref, post_ref, out_ref):
    total = (a_ref[...].astype(F32) + b_ref[...].astype(F32)) + (
        c_ref[...].astype(F32) + d_ref[...].astype(F32)
    )
    out_ref[...] = (residual_ref[...] + rms_scale(total, post_ref[...])).astype(BF16)


def mlp_kernel(rows_ref, weights_ref, out_ref, hidden_ref):
    rows = rows_ref[...]
    units = weights_ref.shape[1]
    last = (((1,), (1,)), ((), ()))
    for i in range(2):
        gate_part = lax.dot_general(rows, weights_ref[3 * i], last, preferred_element_type=F32)
        up_part = lax.dot_general(rows, weights_ref[3 * i + 1], last, preferred_element_type=F32)
        hidden_ref[:, i * units:(i + 1) * units] = (
            jax.nn.gelu(gate_part, approximate=True) * up_part
        ).astype(BF16)
    width = out_ref.shape[1]
    for n in range(0, width, 512):
        total = jnp.dot(
            hidden_ref[:, :units], weights_ref[2, :, n:n + 512], preferred_element_type=F32
        ) + jnp.dot(
            hidden_ref[:, units:], weights_ref[5, :, n:n + 512], preferred_element_type=F32
        )
        out_ref[:, n:n + 512] = total.astype(out_ref.dtype)


def mlp(rows, weights, out_type):
    count, width = rows.shape
    units = weights.shape[1]
    vmem = pl.BlockSpec(memory_space=pltpu.VMEM)
    return pl.pallas_call(
        mlp_kernel,
        out_shape=jax.ShapeDtypeStruct((count, width), out_type),
        in_specs=[vmem] * 2,
        out_specs=vmem,
        scratch_shapes=[pltpu.VMEM((count, 2 * units), BF16)],
        cost_estimate=pl.CostEstimate(
            flops=12 * count * width * units,
            transcendentals=2 * count * units,
            bytes_accessed=4 * count * width,
        ),
        compiler_params=small(MLP_MIB),
        name="mlp",
    )(rows, weights)


def local(
    tokens,
    segment_ids,
    past_len,
    page_table,
    migrate_pages,
    pooled_key_cache,
    pooled_value_cache,
    attn_gain,
    w_query,
    key_matrix,
    value_matrix,
    w_out,
    post_attn_gain,
    ffw_gain,
    w_gate,
    w_up,
    w_down,
    post_ffw_gain,
):
    tok_count, width = tokens.shape
    here = lax.axis_index("mlp")
    other = [(0, 1), (1, 0)]

    packed = pick_pages(migrate_pages.reshape(-1), pooled_key_cache, pooled_value_cache)
    received = lax.all_to_all(packed, REQ, split_axis=0, concat_axis=0, tiled=True)

    gate, up = w_gate.T, w_up.T
    weights = (gate, up, w_down) + tuple(
        lax.ppermute(w, "core", other) for w in (gate, up, w_down)
    )

    segment = segment_ids[0]
    past = past_len[0]
    offsets, token_positions = token_layout(segment, past)
    normalized_input = rms_scale(tokens.astype(F32), attn_gain).astype(BF16)
    query_rows = apply_rotary(
        jnp.dot(normalized_input, w_query, preferred_element_type=F32).reshape(
            tok_count, HEADS, HEAD_SIZE
        ),
        token_positions,
    ).astype(BF16)
    incoming_keys = apply_rotary(
        jnp.dot(normalized_input, key_matrix, preferred_element_type=F32).reshape(
            tok_count, 1, HEAD_SIZE
        ),
        token_positions,
    ).astype(BF16).reshape(tok_count, HEAD_SIZE)
    incoming_values = jnp.dot(
        normalized_input, value_matrix, preferred_element_type=F32
    ).astype(BF16)

    page_ids = jnp.arange(2 * POOL, dtype=jnp.int32)
    place = jnp.sum(
        jnp.where(page_table[0][None, :] == page_ids[:, None], page_ids[None, :], 0), axis=1
    )
    page_req = place // WIN_PAGES
    page_past = jnp.sum(
        jnp.where(page_req[:, None] == jnp.arange(4, dtype=jnp.int32)[None, :], past[None, :], 0),
        axis=1,
    )
    slot = (place % WIN_PAGES * PAGE)[:, None] + jnp.arange(PAGE, dtype=jnp.int32)[None, :]
    code = jnp.where(
        slot >= WINDOW_LENGTH - page_past[:, None], page_req[:, None] * 4096 + slot, -1
    ).reshape(1, -1)

    order = (jnp.arange(tok_count, dtype=jnp.int32) + here * ROWS) % tok_count
    turn = lambda v: lax.dynamic_slice_in_dim(jnp.concatenate([v, v], 0), here * ROWS, tok_count, 0)
    low = turn(segment * 4096 + offsets)[:, None]
    high = turn(segment * 4096 + WINDOW_LENGTH)[:, None]
    query = turn(query_rows).transpose(1, 0, 2)
    own_rows = lax.dynamic_slice_in_dim(tokens, here * ROWS, ROWS, 0)

    acc, total = own_attention(
        low, high, order[:, None], segment[None, :], query, incoming_keys, incoming_values,
        code[:, : POOL * PAGE], pooled_key_cache, pooled_value_cache,
    )
    parts = far_attention(
        low, high, query, code[:, POOL * PAGE:], acc, total, received, w_out, 4
    )
    weights, *parts = lax.optimization_barrier((weights, *parts))
    weights = load_weights(weights)
    for k in range(1, 4):
        parts[k] = lax.ppermute(parts[k], "mlp", [(i, (i + k) % 4) for i in range(4)])
    vmem = pl.BlockSpec(memory_space=pltpu.VMEM)
    residual, entering = pl.pallas_call(
        enter_kernel,
        out_shape=(
            jax.ShapeDtypeStruct((ROWS, width), F32),
            jax.ShapeDtypeStruct((ROWS, width), BF16),
        ),
        in_specs=[vmem] * 7,
        out_specs=(vmem, vmem),
        compiler_params=small(6),
        name="enter",
    )(own_rows, *parts, post_attn_gain[None, :], ffw_gain[None, :])

    line = jnp.concatenate([entering] + [shift(entering, True, k) for k in (1, 2, 3)], axis=0)
    near_out = mlp(line, weights, F32)
    sides = jnp.concatenate([shift(line, False, k) for k in (1, 3)], axis=0)
    across = shift(line, False, 2)
    side_out = mlp(sides, weights, BF16)
    across_out = mlp(across, weights, BF16)
    step = 4 * ROWS
    back = [shift(side_out[:step], False, -1), shift(side_out[step:], False, -3), shift(across_out, False, -2)]
    line_out = near_out + sum(b.astype(F32) for b in back)
    line_out = line_out.astype(BF16)
    ends = [line_out[:ROWS]] + [
        shift(line_out[k * ROWS:(k + 1) * ROWS], True, -k) for k in (1, 2, 3)
    ]
    mixed = pl.pallas_call(
        leave_kernel,
        out_shape=jax.ShapeDtypeStruct((ROWS, width), BF16),
        in_specs=[vmem] * 6,
        out_specs=vmem,
        compiler_params=small(6),
        name="leave",
    )(residual, *ends, post_ffw_gain[None, :])
    return (mixed, incoming_keys, incoming_values)


def solution(mesh):
    chips = Mesh(mesh.devices.reshape(4, 4, 2, 4), ("x", "z", "core", "mlp"))
    return jax.shard_map(
        local,
        mesh=chips,
        in_specs=(
            P(REQ, None),
            P(REQ, None),
            P(REQ, None),
            P(REQ, None),
            P(REQ, None, None),
            P(REQ, None, "mlp"),
            P(REQ, None, "mlp"),
            P(),
            P(None, "mlp"),
            P(None, "mlp"),
            P(None, "mlp"),
            P("mlp", None),
            P(),
            P(),
            P(None, REQ),
            P(None, REQ),
            P(REQ, None),
            P(),
        ),
        out_specs=(P((*REQ, "mlp"), None), P(REQ, "mlp"), P(REQ, "mlp")),
        check_vma=False,
    )
```

```python
import jax
import jax.numpy as jnp
from jax import lax
from jax.experimental import pallas as pl
from jax.experimental.pallas import tpu as pltpu
from jax.sharding import Mesh, PartitionSpec as P

HEAD_SIZE = 256
WINDOW_LENGTH = 1024
PAGE = 64
WIN_PAGES = 16
OWNERS = 32
POOL = 32
HEADS = 2
ROWS = 32

SOFT_CAP = 50.0
NORM_EPS = 1e-06
ROPE_BASE = 10000.0
MLP_MIB = 8
LOAD_MIB = 4
FAR_MIB = 58

BF16 = jnp.bfloat16
F32 = jnp.float32

REQ = ("x", "z", "core")


def rms_scale(values, gain):
    return values * lax.rsqrt(jnp.mean(values * values, axis=-1, keepdims=True) + NORM_EPS) * gain


def apply_rotary(vectors, token_positions):
    half = HEAD_SIZE // 2
    frequency = ROPE_BASE ** (-jnp.arange(half, dtype=F32) * (2.0 / HEAD_SIZE))
    angles = token_positions.astype(F32)[:, None] * frequency[None, :]
    cosine = jnp.cos(angles)[:, None, :]
    sine = jnp.sin(angles)[:, None, :]
    first = vectors[..., :half]
    second = vectors[..., half:]
    return jnp.concatenate(
        [first * cosine - second * sine, second * cosine + first * sine], axis=-1
    )


def token_layout(segment, past):
    requests = jnp.arange(past.shape[0], dtype=jnp.int32)
    member = segment[:, None] == requests[None, :]
    firsts = jnp.sum((segment[:, None] < requests[None, :]).astype(jnp.int32), axis=0)
    offsets = jnp.arange(segment.shape[0], dtype=jnp.int32) - jnp.sum(
        jnp.where(member, firsts[None, :], 0), axis=1
    )
    token_positions = jnp.sum(jnp.where(member, past[None, :], 0), axis=1) + offsets
    return (offsets, token_positions)


def chip_shift(first, k):
    pairs = []
    for x in range(4):
        for z in range(4):
            for c in range(2):
                if (c == 0) == first:
                    to = ((x + k) % 4, z)
                else:
                    to = (x, (z + k) % 4)
                pairs.append(((x * 4 + z) * 2 + c, (to[0] * 4 + to[1]) * 2 + c))
    return pairs


def shift(value, first, k):
    return lax.ppermute(value, REQ, chip_shift(first, k % 4))


def small(megabytes):
    return pltpu.CompilerParams(vmem_limit_bytes=megabytes * 1024 * 1024)


GROUP = 8


def pick_pages_kernel(pages_ref, keys_ref, values_ref, out_ref, keys_held, values_held, held_ref,
                      in_sems, out_sems):
    loads = []
    for g in range(POOL // GROUP):
        part = pl.ds(g * GROUP, GROUP)
        loads.append(pltpu.make_async_copy(keys_ref.at[part], keys_held.at[part], in_sems.at[0, g]))
        loads.append(pltpu.make_async_copy(values_ref.at[part], values_held.at[part], in_sems.at[1, g]))
    for load in loads:
        load.start()
    for load in loads:
        load.wait()
    stores = []
    for g in range(OWNERS // GROUP):
        for d in range(g * GROUP, (g + 1) * GROUP):
            page = pages_ref[d]
            held_ref[d, 0] = keys_held[page]
            held_ref[d, 1] = values_held[page]
        part = pl.ds(g * GROUP, GROUP)
        stores.append(pltpu.make_async_copy(held_ref.at[part], out_ref.at[part], out_sems.at[g]))
        stores[-1].start()
    for store in stores:
        store.wait()


def pick_pages(pages, keys, values):
    hbm = pl.BlockSpec(memory_space=pltpu.HBM)
    return pl.pallas_call(
        pick_pages_kernel,
        out_shape=jax.ShapeDtypeStruct((OWNERS, 2, PAGE, HEAD_SIZE), BF16),
        grid_spec=pltpu.PrefetchScalarGridSpec(
            num_scalar_prefetch=1,
            grid=(),
            in_specs=[hbm] * 2,
            out_specs=hbm,
            scratch_shapes=[
                pltpu.VMEM((POOL, PAGE, HEAD_SIZE), BF16),
                pltpu.VMEM((POOL, PAGE, HEAD_SIZE), BF16),
                pltpu.VMEM((OWNERS, 2, PAGE, HEAD_SIZE), BF16),
                pltpu.SemaphoreType.DMA((2, POOL // GROUP)),
                pltpu.SemaphoreType.DMA((OWNERS // GROUP,)),
            ],
        ),
        compiler_params=small(56),
        name="pick_pages",
    )(pages, keys, values)


def load_kernel(*refs):
    *weights, out_ref, sems = refs
    copies = [
        pltpu.make_async_copy(w, out_ref.at[i], sems.at[i]) for i, w in enumerate(weights)
    ]
    for copy in copies:
        copy.start()
    for copy in copies:
        copy.wait()


def load_weights(weights):
    units, width = weights[0].shape
    count = len(weights)
    return pl.pallas_call(
        load_kernel,
        out_shape=pltpu.VMEM((count, units, width), BF16),
        in_specs=[pl.BlockSpec(memory_space=pltpu.HBM)] * count,
        out_specs=pl.BlockSpec(memory_space=pltpu.VMEM),
        scratch_shapes=[pltpu.SemaphoreType.DMA((count,))],
        cost_estimate=pl.CostEstimate(
            flops=0, transcendentals=0, bytes_accessed=2 * count * units * width
        ),
        compiler_params=small(LOAD_MIB),
        name="load_weights",
    )(*weights)


def attend(query, keys, values, visible, acc_ref, total_ref):
    scores = lax.dot_general(
        query, keys, (((1,), (1,)), ((), ())), preferred_element_type=F32
    )
    raw = jnp.exp(SOFT_CAP * jnp.tanh(scores * (1.0 / (16.0 * SOFT_CAP))))
    weight = jnp.where(jnp.concatenate([visible] * HEADS, axis=0), raw, 0.0)
    total_ref[...] += jnp.broadcast_to(jnp.sum(weight, axis=-1, keepdims=True), total_ref.shape)
    acc_ref[...] += jnp.dot(weight.astype(BF16), values, preferred_element_type=F32)


STEP_PAGES = 8
STEP = STEP_PAGES * PAGE


def own_kernel(low_ref, high_ref, order_ref, seg_row_ref, query_ref, new_keys_ref, new_values_ref,
               code_ref, keys_ref, values_ref, acc_ref, total_ref):
    acc_ref[...] = jnp.zeros_like(acc_ref)
    total_ref[...] = jnp.zeros_like(total_ref)
    low, high, order = low_ref[...], high_ref[...], order_ref[...]
    count = order.shape[0]
    column = lax.broadcasted_iota(jnp.int32, (count, count), 1)
    same = lax.div(high, 4096) == seg_row_ref[...]
    attend(query_ref[...], new_keys_ref[...], new_values_ref[...], same & (column <= order), acc_ref, total_ref)
    for b in range(POOL // STEP_PAGES):
        keys = keys_ref[b * STEP_PAGES:(b + 1) * STEP_PAGES].reshape(STEP, HEAD_SIZE)
        values = values_ref[b * STEP_PAGES:(b + 1) * STEP_PAGES].reshape(STEP, HEAD_SIZE)
        code = code_ref[:, b * STEP:(b + 1) * STEP]
        attend(query_ref[...], keys, values, (code > low) & (code < high), acc_ref, total_ref)


def own_attention(low, high, order, seg_row, query, new_keys, new_values, code, keys, values):
    vmem = pl.BlockSpec(memory_space=pltpu.VMEM)
    return pl.pallas_call(
        own_kernel,
        out_shape=(
            jax.ShapeDtypeStruct((HEADS * 128, HEAD_SIZE), F32),
            jax.ShapeDtypeStruct((HEADS * 128, 128), F32),
        ),
        in_specs=[vmem] * 10,
        out_specs=(vmem, vmem),
        cost_estimate=pl.CostEstimate(
            flops=4 * 256 * 2176 * 256, transcendentals=2 * 256 * 2176, bytes_accessed=3_000_000
        ),
        compiler_params=small(10),
        name="own_attention",
    )(low, high, order, seg_row, query, new_keys, new_values, code, keys, values)


def far_kernel(low_hbm, high_hbm, code_hbm, query_hbm, acc_hbm, total_hbm, pages_ref, w_hbm, *refs):
    (*out_refs, acc_ref, total_ref, query_ref, acc_in_ref, total_in_ref, held_ref, w_ref,
     low_ref, high_ref, code_ref, page_sems, sems) = refs
    blocks = OWNERS // STEP_PAGES
    loads = [
        pltpu.make_async_copy(
            pages_ref.at[b * STEP_PAGES:(b + 1) * STEP_PAGES], held_ref.at[b], page_sems.at[b]
        )
        for b in range(blocks)
    ]
    query_load = pltpu.make_async_copy(query_hbm, query_ref, sems.at[0])
    acc_load = pltpu.make_async_copy(acc_hbm, acc_in_ref, sems.at[1])
    total_load = pltpu.make_async_copy(total_hbm, total_in_ref, sems.at[2])
    w_load = pltpu.make_async_copy(w_hbm, w_ref, sems.at[3])
    small_loads = [
        pltpu.make_async_copy(low_hbm, low_ref, sems.at[4]),
        pltpu.make_async_copy(high_hbm, high_ref, sems.at[5]),
        pltpu.make_async_copy(code_hbm, code_ref, sems.at[6]),
        query_load,
    ]
    for load in small_loads:
        load.start()
    for load in loads:
        load.start()
    acc_ref[...] = jnp.zeros_like(acc_ref)
    total_ref[...] = jnp.zeros_like(total_ref)
    for load in small_loads:
        load.wait()
    low, high = low_ref[...], high_ref[...]
    for b in range(blocks):
        loads[b].wait()
        if b == 0:
            w_load.start()
            acc_load.start()
            total_load.start()
        keys = held_ref[b, :, 0].reshape(STEP, HEAD_SIZE)
        values = held_ref[b, :, 1].reshape(STEP, HEAD_SIZE)
        code = code_ref[:, b * STEP:(b + 1) * STEP]
        attend(query_ref[...], keys, values, (code > low) & (code < high), acc_ref, total_ref)
    acc_load.wait()
    total_load.wait()
    heads = (
        (acc_ref[...] + acc_in_ref[...]) / (total_ref[...] + total_in_ref[...])[:, :1]
    ).astype(BF16)
    attention = jnp.concatenate([heads[h * 128:(h + 1) * 128] for h in range(HEADS)], axis=1)
    rows, width = out_refs[0].shape
    w_load.wait()
    for n in range(0, width, 512):
        block = jnp.dot(
            attention, w_ref[:, n:n + 512], preferred_element_type=F32
        ).astype(BF16)
        for i, out_ref in enumerate(out_refs):
            out_ref[:, n:n + 512] = block[i * rows:(i + 1) * rows]


def far_attention(low, high, query, code, acc, total, pages, w_out, blocks):
    vmem = pl.BlockSpec(memory_space=pltpu.VMEM)
    hbm = pl.BlockSpec(memory_space=pltpu.HBM)
    width = w_out.shape[1]
    return pl.pallas_call(
        far_kernel,
        out_shape=[pltpu.VMEM((128 // blocks, width), BF16)] * blocks,
        in_specs=[hbm] * 8,
        out_specs=[vmem] * blocks,
        scratch_shapes=[
            pltpu.VMEM((HEADS * 128, HEAD_SIZE), F32),
            pltpu.VMEM((HEADS * 128, 128), F32),
            pltpu.VMEM((HEADS * 128, HEAD_SIZE), BF16),
            pltpu.VMEM((HEADS * 128, HEAD_SIZE), F32),
            pltpu.VMEM((HEADS * 128, 128), F32),
            pltpu.VMEM((OWNERS // STEP_PAGES, STEP_PAGES, 2, PAGE, HEAD_SIZE), BF16),
            pltpu.VMEM(w_out.shape, BF16),
            pltpu.VMEM(low.shape, jnp.int32),
            pltpu.VMEM(high.shape, jnp.int32),
            pltpu.VMEM(code.shape, jnp.int32),
            pltpu.SemaphoreType.DMA((OWNERS // STEP_PAGES,)),
            pltpu.SemaphoreType.DMA((7,)),
        ],
        cost_estimate=pl.CostEstimate(
            flops=4 * 256 * 2048 * 256, transcendentals=2 * 256 * 2048, bytes_accessed=7_000_000
        ),
        compiler_params=small(FAR_MIB),
        name="far_attention",
    )(low, high, code, query, acc, total, pages, w_out)


def enter_kernel(own_ref, a_ref, b_ref, c_ref, d_ref, post_ref, ffw_ref, residual_ref, out_ref):
    total = (a_ref[...].astype(F32) + b_ref[...].astype(F32)) + (
        c_ref[...].astype(F32) + d_ref[...].astype(F32)
    )
    residual = own_ref[...].astype(F32) + rms_scale(total, post_ref[...])
    residual_ref[...] = residual
    out_ref[...] = rms_scale(residual, ffw_ref[...]).astype(BF16)


def leave_kernel(residual_ref, a_ref, b_ref, c_ref, d_ref, post_ref, out_ref):
    total = (a_ref[...].astype(F32) + b_ref[...].astype(F32)) + (
        c_ref[...].astype(F32) + d_ref[...].astype(F32)
    )
    out_ref[...] = (residual_ref[...] + rms_scale(total, post_ref[...])).astype(BF16)


def mlp_kernel(rows_ref, weights_ref, out_ref, hidden_ref):
    rows = rows_ref[...]
    units = weights_ref.shape[1]
    last = (((1,), (1,)), ((), ()))
    for i in range(2):
        gate_part = lax.dot_general(rows, weights_ref[3 * i], last, preferred_element_type=F32)
        up_part = lax.dot_general(rows, weights_ref[3 * i + 1], last, preferred_element_type=F32)
        hidden_ref[:, i * units:(i + 1) * units] = (
            jax.nn.gelu(gate_part, approximate=True) * up_part
        ).astype(BF16)
    width = out_ref.shape[1]
    for n in range(0, width, 512):
        total = jnp.dot(
            hidden_ref[:, :units], weights_ref[2, :, n:n + 512], preferred_element_type=F32
        ) + jnp.dot(
            hidden_ref[:, units:], weights_ref[5, :, n:n + 512], preferred_element_type=F32
        )
        out_ref[:, n:n + 512] = total.astype(out_ref.dtype)


def mlp(rows, weights, out_type):
    count, width = rows.shape
    units = weights.shape[1]
    vmem = pl.BlockSpec(memory_space=pltpu.VMEM)
    return pl.pallas_call(
        mlp_kernel,
        out_shape=jax.ShapeDtypeStruct((count, width), out_type),
        in_specs=[vmem] * 2,
        out_specs=vmem,
        scratch_shapes=[pltpu.VMEM((count, 2 * units), BF16)],
        cost_estimate=pl.CostEstimate(
            flops=12 * count * width * units,
            transcendentals=2 * count * units,
            bytes_accessed=4 * count * width,
        ),
        compiler_params=small(MLP_MIB),
        name="mlp",
    )(rows, weights)


def local(
    tokens,
    segment_ids,
    past_len,
    page_table,
    migrate_pages,
    pooled_key_cache,
    pooled_value_cache,
    attn_gain,
    w_query,
    key_matrix,
    value_matrix,
    w_out,
    post_attn_gain,
    ffw_gain,
    w_gate,
    w_up,
    w_down,
    post_ffw_gain,
):
    tok_count, width = tokens.shape
    here = lax.axis_index("mlp")
    other = [(0, 1), (1, 0)]

    packed = pick_pages(migrate_pages.reshape(-1), pooled_key_cache, pooled_value_cache)

    gate, up = w_gate.T, w_up.T
    packed, *sent = lax.optimization_barrier((packed, gate, up, w_down))
    received = lax.all_to_all(packed, REQ, split_axis=0, concat_axis=0, tiled=True)
    weights = (gate, up, w_down) + tuple(lax.ppermute(w, "core", other) for w in sent)

    segment = segment_ids[0]
    past = past_len[0]
    offsets, token_positions = token_layout(segment, past)
    normalized_input = rms_scale(tokens.astype(F32), attn_gain).astype(BF16)
    query_rows = apply_rotary(
        jnp.dot(normalized_input, w_query, preferred_element_type=F32).reshape(
            tok_count, HEADS, HEAD_SIZE
        ),
        token_positions,
    ).astype(BF16)
    incoming_keys = apply_rotary(
        jnp.dot(normalized_input, key_matrix, preferred_element_type=F32).reshape(
            tok_count, 1, HEAD_SIZE
        ),
        token_positions,
    ).astype(BF16).reshape(tok_count, HEAD_SIZE)
    incoming_values = jnp.dot(
        normalized_input, value_matrix, preferred_element_type=F32
    ).astype(BF16)

    page_ids = jnp.arange(2 * POOL, dtype=jnp.int32)
    place = jnp.sum(
        jnp.where(page_table[0][None, :] == page_ids[:, None], page_ids[None, :], 0), axis=1
    )
    page_req = place // WIN_PAGES
    page_past = jnp.sum(
        jnp.where(page_req[:, None] == jnp.arange(4, dtype=jnp.int32)[None, :], past[None, :], 0),
        axis=1,
    )
    slot = (place % WIN_PAGES * PAGE)[:, None] + jnp.arange(PAGE, dtype=jnp.int32)[None, :]
    code = jnp.where(
        slot >= WINDOW_LENGTH - page_past[:, None], page_req[:, None] * 4096 + slot, -1
    ).reshape(1, -1)

    order = (jnp.arange(tok_count, dtype=jnp.int32) + here * ROWS) % tok_count
    turn = lambda v: lax.dynamic_slice_in_dim(jnp.concatenate([v, v], 0), here * ROWS, tok_count, 0)
    low = turn(segment * 4096 + offsets)[:, None]
    high = turn(segment * 4096 + WINDOW_LENGTH)[:, None]
    query = turn(query_rows).transpose(1, 0, 2).reshape(HEADS * tok_count, HEAD_SIZE)
    own_rows = lax.dynamic_slice_in_dim(tokens, here * ROWS, ROWS, 0)

    acc, total = own_attention(
        low, high, order[:, None], segment[None, :], query, incoming_keys, incoming_values,
        code[:, : POOL * PAGE], pooled_key_cache, pooled_value_cache,
    )
    parts = far_attention(
        low, high, query, code[:, POOL * PAGE:], acc, total, received, w_out, 4
    )
    weights, *parts = lax.optimization_barrier((weights, *parts))
    weights = load_weights(weights)
    for k in range(1, 4):
        parts[k] = lax.ppermute(parts[k], "mlp", [(i, (i + k) % 4) for i in range(4)])
    vmem = pl.BlockSpec(memory_space=pltpu.VMEM)
    residual, entering = pl.pallas_call(
        enter_kernel,
        out_shape=(
            jax.ShapeDtypeStruct((ROWS, width), F32),
            jax.ShapeDtypeStruct((ROWS, width), BF16),
        ),
        in_specs=[vmem] * 7,
        out_specs=(vmem, vmem),
        compiler_params=small(6),
        name="enter",
    )(own_rows, *parts, post_attn_gain[None, :], ffw_gain[None, :])

    line = jnp.concatenate([entering] + [shift(entering, True, k) for k in (1, 2, 3)], axis=0)
    near_out = mlp(line, weights, F32)
    sides = jnp.concatenate([shift(line, False, k) for k in (1, 3)], axis=0)
    across = shift(line, False, 2)
    side_out = mlp(sides, weights, BF16)
    across_out = mlp(across, weights, BF16)
    step = 4 * ROWS
    back = [shift(side_out[:step], False, -1), shift(side_out[step:], False, -3), shift(across_out, False, -2)]
    line_out = near_out + sum(b.astype(F32) for b in back)
    line_out = line_out.astype(BF16)
    ends = [line_out[:ROWS]] + [
        shift(line_out[k * ROWS:(k + 1) * ROWS], True, -k) for k in (1, 2, 3)
    ]
    mixed = pl.pallas_call(
        leave_kernel,
        out_shape=jax.ShapeDtypeStruct((ROWS, width), BF16),
        in_specs=[vmem] * 6,
        out_specs=vmem,
        compiler_params=small(6),
        name="leave",
    )(residual, *ends, post_ffw_gain[None, :])
    return (mixed, incoming_keys, incoming_values)


def solution(mesh):
    chips = Mesh(mesh.devices.reshape(4, 4, 2, 4), ("x", "z", "core", "mlp"))
    return jax.shard_map(
        local,
        mesh=chips,
        in_specs=(
            P(REQ, None),
            P(REQ, None),
            P(REQ, None),
            P(REQ, None),
            P(REQ, None, None),
            P(REQ, None, "mlp"),
            P(REQ, None, "mlp"),
            P(),
            P(None, "mlp"),
            P(None, "mlp"),
            P(None, "mlp"),
            P("mlp", None),
            P(),
            P(),
            P(None, REQ),
            P(None, REQ),
            P(REQ, None),
            P(),
        ),
        out_specs=(P((*REQ, "mlp"), None), P(REQ, "mlp"), P(REQ, "mlp")),
        check_vma=False,
    )
```

```python
import jax
import jax.numpy as jnp
from jax import lax
from jax.experimental import pallas as pl
from jax.experimental.pallas import tpu as pltpu
from jax.sharding import Mesh, PartitionSpec as P

HEAD_SIZE = 256
WINDOW_LENGTH = 1024
PAGE = 64
WIN_PAGES = 16
OWNERS = 32
POOL = 32
HEADS = 2
ROWS = 32

SOFT_CAP = 50.0
NORM_EPS = 1e-06
ROPE_BASE = 10000.0
MLP_MIB = 8
LOAD_MIB = 4
FAR_MIB = 58

BF16 = jnp.bfloat16
F32 = jnp.float32

REQ = ("x", "z", "core")


def rms_scale(values, gain):
    return values * lax.rsqrt(jnp.mean(values * values, axis=-1, keepdims=True) + NORM_EPS) * gain


def apply_rotary(vectors, token_positions):
    half = HEAD_SIZE // 2
    frequency = ROPE_BASE ** (-jnp.arange(half, dtype=F32) * (2.0 / HEAD_SIZE))
    angles = token_positions.astype(F32)[:, None] * frequency[None, :]
    cosine = jnp.cos(angles)[:, None, :]
    sine = jnp.sin(angles)[:, None, :]
    first = vectors[..., :half]
    second = vectors[..., half:]
    return jnp.concatenate(
        [first * cosine - second * sine, second * cosine + first * sine], axis=-1
    )


def token_layout(segment, past):
    requests = jnp.arange(past.shape[0], dtype=jnp.int32)
    member = segment[:, None] == requests[None, :]
    firsts = jnp.sum((segment[:, None] < requests[None, :]).astype(jnp.int32), axis=0)
    offsets = jnp.arange(segment.shape[0], dtype=jnp.int32) - jnp.sum(
        jnp.where(member, firsts[None, :], 0), axis=1
    )
    token_positions = jnp.sum(jnp.where(member, past[None, :], 0), axis=1) + offsets
    return (offsets, token_positions)


def chip_shift(first, k):
    pairs = []
    for x in range(4):
        for z in range(4):
            for c in range(2):
                if (c == 0) == first:
                    to = ((x + k) % 4, z)
                else:
                    to = (x, (z + k) % 4)
                pairs.append(((x * 4 + z) * 2 + c, (to[0] * 4 + to[1]) * 2 + c))
    return pairs


def shift(value, first, k):
    return lax.ppermute(value, REQ, chip_shift(first, k % 4))


def small(megabytes):
    return pltpu.CompilerParams(vmem_limit_bytes=megabytes * 1024 * 1024)


GROUP = 4


def pick_pages_kernel(pages_ref, keys_ref, values_ref, out_ref, keys_held, values_held, held_ref,
                      in_sems, out_sems):
    loads = []
    for g in range(POOL // GROUP):
        part = pl.ds(g * GROUP, GROUP)
        loads.append(pltpu.make_async_copy(keys_ref.at[part], keys_held.at[part], in_sems.at[0, g]))
        loads.append(pltpu.make_async_copy(values_ref.at[part], values_held.at[part], in_sems.at[1, g]))
    for load in loads:
        load.start()
    for load in loads:
        load.wait()
    stores = []
    for g in range(OWNERS // GROUP):
        for d in range(g * GROUP, (g + 1) * GROUP):
            page = pages_ref[d]
            held_ref[d, 0] = keys_held[page]
            held_ref[d, 1] = values_held[page]
        part = pl.ds(g * GROUP, GROUP)
        stores.append(pltpu.make_async_copy(held_ref.at[part], out_ref.at[part], out_sems.at[g]))
        stores[-1].start()
    for store in stores:
        store.wait()


def pick_pages(pages, keys, values):
    hbm = pl.BlockSpec(memory_space=pltpu.HBM)
    return pl.pallas_call(
        pick_pages_kernel,
        out_shape=jax.ShapeDtypeStruct((OWNERS, 2, PAGE, HEAD_SIZE), BF16),
        grid_spec=pltpu.PrefetchScalarGridSpec(
            num_scalar_prefetch=1,
            grid=(),
            in_specs=[hbm] * 2,
            out_specs=hbm,
            scratch_shapes=[
                pltpu.VMEM((POOL, PAGE, HEAD_SIZE), BF16),
                pltpu.VMEM((POOL, PAGE, HEAD_SIZE), BF16),
                pltpu.VMEM((OWNERS, 2, PAGE, HEAD_SIZE), BF16),
                pltpu.SemaphoreType.DMA((2, POOL // GROUP)),
                pltpu.SemaphoreType.DMA((OWNERS // GROUP,)),
            ],
        ),
        compiler_params=small(56),
        name="pick_pages",
    )(pages, keys, values)


def load_kernel(*refs):
    *weights, out_ref, sems = refs
    copies = [
        pltpu.make_async_copy(w, out_ref.at[i], sems.at[i]) for i, w in enumerate(weights)
    ]
    for copy in copies:
        copy.start()
    for copy in copies:
        copy.wait()


def load_weights(weights):
    units, width = weights[0].shape
    count = len(weights)
    return pl.pallas_call(
        load_kernel,
        out_shape=pltpu.VMEM((count, units, width), BF16),
        in_specs=[pl.BlockSpec(memory_space=pltpu.HBM)] * count,
        out_specs=pl.BlockSpec(memory_space=pltpu.VMEM),
        scratch_shapes=[pltpu.SemaphoreType.DMA((count,))],
        cost_estimate=pl.CostEstimate(
            flops=0, transcendentals=0, bytes_accessed=2 * count * units * width
        ),
        compiler_params=small(LOAD_MIB),
        name="load_weights",
    )(*weights)


def attend(query, keys, values, visible, acc_ref, total_ref):
    scores = lax.dot_general(
        query, keys, (((1,), (1,)), ((), ())), preferred_element_type=F32
    )
    raw = jnp.exp(SOFT_CAP * jnp.tanh(scores * (1.0 / (16.0 * SOFT_CAP))))
    weight = jnp.where(jnp.concatenate([visible] * HEADS, axis=0), raw, 0.0)
    total_ref[...] += jnp.broadcast_to(jnp.sum(weight, axis=-1, keepdims=True), total_ref.shape)
    acc_ref[...] += jnp.dot(weight.astype(BF16), values, preferred_element_type=F32)


STEP_PAGES = 8
STEP = STEP_PAGES * PAGE


def own_kernel(low_ref, high_ref, order_ref, seg_row_ref, query_ref, new_keys_ref, new_values_ref,
               code_ref, keys_ref, values_ref, acc_ref, total_ref):
    acc_ref[...] = jnp.zeros_like(acc_ref)
    total_ref[...] = jnp.zeros_like(total_ref)
    low, high, order = low_ref[...], high_ref[...], order_ref[...]
    count = order.shape[0]
    column = lax.broadcasted_iota(jnp.int32, (count, count), 1)
    same = lax.div(high, 4096) == seg_row_ref[...]
    attend(query_ref[...], new_keys_ref[...], new_values_ref[...], same & (column <= order), acc_ref, total_ref)
    for b in range(POOL // STEP_PAGES):
        keys = keys_ref[b * STEP_PAGES:(b + 1) * STEP_PAGES].reshape(STEP, HEAD_SIZE)
        values = values_ref[b * STEP_PAGES:(b + 1) * STEP_PAGES].reshape(STEP, HEAD_SIZE)
        code = code_ref[:, b * STEP:(b + 1) * STEP]
        attend(query_ref[...], keys, values, (code > low) & (code < high), acc_ref, total_ref)


def own_attention(low, high, order, seg_row, query, new_keys, new_values, code, keys, values):
    vmem = pl.BlockSpec(memory_space=pltpu.VMEM)
    return pl.pallas_call(
        own_kernel,
        out_shape=(
            jax.ShapeDtypeStruct((HEADS * 128, HEAD_SIZE), F32),
            jax.ShapeDtypeStruct((HEADS * 128, 128), F32),
        ),
        in_specs=[vmem] * 10,
        out_specs=(vmem, vmem),
        cost_estimate=pl.CostEstimate(
            flops=4 * 256 * 2176 * 256, transcendentals=2 * 256 * 2176, bytes_accessed=3_000_000
        ),
        compiler_params=small(10),
        name="own_attention",
    )(low, high, order, seg_row, query, new_keys, new_values, code, keys, values)


def far_kernel(low_hbm, high_hbm, code_hbm, query_hbm, acc_hbm, total_hbm, pages_ref, w_hbm, *refs):
    (*out_refs, acc_ref, total_ref, query_ref, acc_in_ref, total_in_ref, held_ref, w_ref,
     low_ref, high_ref, code_ref, page_sems, sems) = refs
    blocks = OWNERS // STEP_PAGES
    loads = [
        pltpu.make_async_copy(
            pages_ref.at[b * STEP_PAGES:(b + 1) * STEP_PAGES], held_ref.at[b], page_sems.at[b]
        )
        for b in range(blocks)
    ]
    query_load = pltpu.make_async_copy(query_hbm, query_ref, sems.at[0])
    acc_load = pltpu.make_async_copy(acc_hbm, acc_in_ref, sems.at[1])
    total_load = pltpu.make_async_copy(total_hbm, total_in_ref, sems.at[2])
    w_load = pltpu.make_async_copy(w_hbm, w_ref, sems.at[3])
    small_loads = [
        pltpu.make_async_copy(low_hbm, low_ref, sems.at[4]),
        pltpu.make_async_copy(high_hbm, high_ref, sems.at[5]),
        pltpu.make_async_copy(code_hbm, code_ref, sems.at[6]),
        query_load,
    ]
    for load in small_loads:
        load.start()
    for load in loads:
        load.start()
    for load in (w_load, acc_load, total_load):
        load.start()
    acc_ref[...] = jnp.zeros_like(acc_ref)
    total_ref[...] = jnp.zeros_like(total_ref)
    for load in small_loads:
        load.wait()
    low, high = low_ref[...], high_ref[...]
    for b in range(blocks):
        loads[b].wait()
        keys = held_ref[b, :, 0].reshape(STEP, HEAD_SIZE)
        values = held_ref[b, :, 1].reshape(STEP, HEAD_SIZE)
        code = code_ref[:, b * STEP:(b + 1) * STEP]
        attend(query_ref[...], keys, values, (code > low) & (code < high), acc_ref, total_ref)
    acc_load.wait()
    total_load.wait()
    heads = (
        (acc_ref[...] + acc_in_ref[...]) / (total_ref[...] + total_in_ref[...])[:, :1]
    ).astype(BF16)
    attention = jnp.concatenate([heads[h * 128:(h + 1) * 128] for h in range(HEADS)], axis=1)
    rows, width = out_refs[0].shape
    w_load.wait()
    for n in range(0, width, 512):
        block = jnp.dot(
            attention, w_ref[:, n:n + 512], preferred_element_type=F32
        ).astype(BF16)
        for i, out_ref in enumerate(out_refs):
            out_ref[:, n:n + 512] = block[i * rows:(i + 1) * rows]


def far_attention(low, high, query, code, acc, total, pages, w_out, blocks):
    vmem = pl.BlockSpec(memory_space=pltpu.VMEM)
    hbm = pl.BlockSpec(memory_space=pltpu.HBM)
    width = w_out.shape[1]
    return pl.pallas_call(
        far_kernel,
        out_shape=[pltpu.VMEM((128 // blocks, width), BF16)] * blocks,
        in_specs=[hbm] * 8,
        out_specs=[vmem] * blocks,
        scratch_shapes=[
            pltpu.VMEM((HEADS * 128, HEAD_SIZE), F32),
            pltpu.VMEM((HEADS * 128, 128), F32),
            pltpu.VMEM((HEADS * 128, HEAD_SIZE), BF16),
            pltpu.VMEM((HEADS * 128, HEAD_SIZE), F32),
            pltpu.VMEM((HEADS * 128, 128), F32),
            pltpu.VMEM((OWNERS // STEP_PAGES, STEP_PAGES, 2, PAGE, HEAD_SIZE), BF16),
            pltpu.VMEM(w_out.shape, BF16),
            pltpu.VMEM(low.shape, jnp.int32),
            pltpu.VMEM(high.shape, jnp.int32),
            pltpu.VMEM(code.shape, jnp.int32),
            pltpu.SemaphoreType.DMA((OWNERS // STEP_PAGES,)),
            pltpu.SemaphoreType.DMA((7,)),
        ],
        cost_estimate=pl.CostEstimate(
            flops=4 * 256 * 2048 * 256, transcendentals=2 * 256 * 2048, bytes_accessed=7_000_000
        ),
        compiler_params=small(FAR_MIB),
        name="far_attention",
    )(low, high, code, query, acc, total, pages, w_out)


def enter_kernel(own_ref, a_ref, b_ref, c_ref, d_ref, post_ref, ffw_ref, residual_ref, out_ref):
    total = (a_ref[...].astype(F32) + b_ref[...].astype(F32)) + (
        c_ref[...].astype(F32) + d_ref[...].astype(F32)
    )
    residual = own_ref[...].astype(F32) + rms_scale(total, post_ref[...])
    residual_ref[...] = residual
    out_ref[...] = rms_scale(residual, ffw_ref[...]).astype(BF16)


def leave_kernel(residual_ref, a_ref, b_ref, c_ref, d_ref, post_ref, out_ref):
    total = (a_ref[...].astype(F32) + b_ref[...].astype(F32)) + (
        c_ref[...].astype(F32) + d_ref[...].astype(F32)
    )
    out_ref[...] = (residual_ref[...] + rms_scale(total, post_ref[...])).astype(BF16)


def mlp_kernel(rows_ref, weights_ref, out_ref, hidden_ref):
    rows = rows_ref[...]
    units = weights_ref.shape[1]
    last = (((1,), (1,)), ((), ()))
    for i in range(2):
        gate_part = lax.dot_general(rows, weights_ref[3 * i], last, preferred_element_type=F32)
        up_part = lax.dot_general(rows, weights_ref[3 * i + 1], last, preferred_element_type=F32)
        hidden_ref[:, i * units:(i + 1) * units] = (
            jax.nn.gelu(gate_part, approximate=True) * up_part
        ).astype(BF16)
    width = out_ref.shape[1]
    for n in range(0, width, 512):
        total = jnp.dot(
            hidden_ref[:, :units], weights_ref[2, :, n:n + 512], preferred_element_type=F32
        ) + jnp.dot(
            hidden_ref[:, units:], weights_ref[5, :, n:n + 512], preferred_element_type=F32
        )
        out_ref[:, n:n + 512] = total.astype(out_ref.dtype)


def mlp(rows, weights, out_type):
    count, width = rows.shape
    units = weights.shape[1]
    vmem = pl.BlockSpec(memory_space=pltpu.VMEM)
    return pl.pallas_call(
        mlp_kernel,
        out_shape=jax.ShapeDtypeStruct((count, width), out_type),
        in_specs=[vmem] * 2,
        out_specs=vmem,
        scratch_shapes=[pltpu.VMEM((count, 2 * units), BF16)],
        cost_estimate=pl.CostEstimate(
            flops=12 * count * width * units,
            transcendentals=2 * count * units,
            bytes_accessed=4 * count * width,
        ),
        compiler_params=small(MLP_MIB),
        name="mlp",
    )(rows, weights)


def local(
    tokens,
    segment_ids,
    past_len,
    page_table,
    migrate_pages,
    pooled_key_cache,
    pooled_value_cache,
    attn_gain,
    w_query,
    key_matrix,
    value_matrix,
    w_out,
    post_attn_gain,
    ffw_gain,
    w_gate,
    w_up,
    w_down,
    post_ffw_gain,
):
    tok_count, width = tokens.shape
    here = lax.axis_index("mlp")
    other = [(0, 1), (1, 0)]

    packed = pick_pages(migrate_pages.reshape(-1), pooled_key_cache, pooled_value_cache)

    gate, up = w_gate.T, w_up.T
    packed, *sent = lax.optimization_barrier((packed, gate, up, w_down))
    received = lax.all_to_all(packed, REQ, split_axis=0, concat_axis=0, tiled=True)
    weights = (gate, up, w_down) + tuple(lax.ppermute(w, "core", other) for w in sent)

    segment = segment_ids[0]
    past = past_len[0]
    offsets, token_positions = token_layout(segment, past)
    normalized_input = rms_scale(tokens.astype(F32), attn_gain).astype(BF16)
    query_rows = apply_rotary(
        jnp.dot(normalized_input, w_query, preferred_element_type=F32).reshape(
            tok_count, HEADS, HEAD_SIZE
        ),
        token_positions,
    ).astype(BF16)
    incoming_keys = apply_rotary(
        jnp.dot(normalized_input, key_matrix, preferred_element_type=F32).reshape(
            tok_count, 1, HEAD_SIZE
        ),
        token_positions,
    ).astype(BF16).reshape(tok_count, HEAD_SIZE)
    incoming_values = jnp.dot(
        normalized_input, value_matrix, preferred_element_type=F32
    ).astype(BF16)

    page_ids = jnp.arange(2 * POOL, dtype=jnp.int32)
    place = jnp.sum(
        jnp.where(page_table[0][None, :] == page_ids[:, None], page_ids[None, :], 0), axis=1
    )
    page_req = place // WIN_PAGES
    page_past = jnp.sum(
        jnp.where(page_req[:, None] == jnp.arange(4, dtype=jnp.int32)[None, :], past[None, :], 0),
        axis=1,
    )
    slot = (place % WIN_PAGES * PAGE)[:, None] + jnp.arange(PAGE, dtype=jnp.int32)[None, :]
    code = jnp.where(
        slot >= WINDOW_LENGTH - page_past[:, None], page_req[:, None] * 4096 + slot, -1
    ).reshape(1, -1)

    order = (jnp.arange(tok_count, dtype=jnp.int32) + here * ROWS) % tok_count
    turn = lambda v: lax.dynamic_slice_in_dim(jnp.concatenate([v, v], 0), here * ROWS, tok_count, 0)
    low = turn(segment * 4096 + offsets)[:, None]
    high = turn(segment * 4096 + WINDOW_LENGTH)[:, None]
    query = turn(query_rows).transpose(1, 0, 2).reshape(HEADS * tok_count, HEAD_SIZE)
    own_rows = lax.dynamic_slice_in_dim(tokens, here * ROWS, ROWS, 0)

    acc, total = own_attention(
        low, high, order[:, None], segment[None, :], query, incoming_keys, incoming_values,
        code[:, : POOL * PAGE], pooled_key_cache, pooled_value_cache,
    )
    parts = far_attention(
        low, high, query, code[:, POOL * PAGE:], acc, total, received, w_out, 4
    )
    weights, *parts = lax.optimization_barrier((weights, *parts))
    weights = load_weights(weights)
    for k in range(1, 4):
        parts[k] = lax.ppermute(parts[k], "mlp", [(i, (i + k) % 4) for i in range(4)])
    vmem = pl.BlockSpec(memory_space=pltpu.VMEM)
    residual, entering = pl.pallas_call(
        enter_kernel,
        out_shape=(
            jax.ShapeDtypeStruct((ROWS, width), F32),
            jax.ShapeDtypeStruct((ROWS, width), BF16),
        ),
        in_specs=[vmem] * 7,
        out_specs=(vmem, vmem),
        compiler_params=small(6),
        name="enter",
    )(own_rows, *parts, post_attn_gain[None, :], ffw_gain[None, :])

    line = jnp.concatenate([entering] + [shift(entering, True, k) for k in (1, 2, 3)], axis=0)
    near_out = mlp(line, weights, F32)
    sides = jnp.concatenate([shift(line, False, k) for k in (1, 3)], axis=0)
    across = shift(line, False, 2)
    side_out = mlp(sides, weights, BF16)
    across_out = mlp(across, weights, BF16)
    step = 4 * ROWS
    back = [shift(side_out[:step], False, -1), shift(side_out[step:], False, -3), shift(across_out, False, -2)]
    line_out = near_out + sum(b.astype(F32) for b in back)
    line_out = line_out.astype(BF16)
    ends = [line_out[:ROWS]] + [
        shift(line_out[k * ROWS:(k + 1) * ROWS], True, -k) for k in (1, 2, 3)
    ]
    mixed = pl.pallas_call(
        leave_kernel,
        out_shape=jax.ShapeDtypeStruct((ROWS, width), BF16),
        in_specs=[vmem] * 6,
        out_specs=vmem,
        compiler_params=small(6),
        name="leave",
    )(residual, *ends, post_ffw_gain[None, :])
    return (mixed, incoming_keys, incoming_values)


def solution(mesh):
    chips = Mesh(mesh.devices.reshape(4, 4, 2, 4), ("x", "z", "core", "mlp"))
    return jax.shard_map(
        local,
        mesh=chips,
        in_specs=(
            P(REQ, None),
            P(REQ, None),
            P(REQ, None),
            P(REQ, None),
            P(REQ, None, None),
            P(REQ, None, "mlp"),
            P(REQ, None, "mlp"),
            P(),
            P(None, "mlp"),
            P(None, "mlp"),
            P(None, "mlp"),
            P("mlp", None),
            P(),
            P(),
            P(None, REQ),
            P(None, REQ),
            P(REQ, None),
            P(),
        ),
        out_specs=(P((*REQ, "mlp"), None), P(REQ, "mlp"), P(REQ, "mlp")),
        check_vma=False,
    )
```
